128 devices in a mesh: dp: 8 (over z, y_lo), cp: 16 (over x, y_hi, core).
Axes of the slice: x: 4, y: 4 (y_hi: 2, y_lo: 2; y = y_hi * 2 + y_lo), z: 4, core: 2. Of those that a mesh axis runs over, the one named last changes fastest.
Arguments:
- table_rows: bfloat16 [262144, 1024], P(('dp', 'cp')), may hold values from -6 to 6
- row_scales: float32 [262144], P(('dp', 'cp')), may hold values from 0.25 to 4
- owners: int32 [16384, 1], P(('dp', 'cp')), may hold values from 0 to 127; in each aligned block of 128 rows (0 to 127, 128 to 255, ...) at most 2 rows name the same one
- shard_rows: int32 [16384], P(('dp', 'cp')), may hold values from 0 to 2047
- history_lengths: int32 [8, 3], P('dp'), may hold values from 1 to 1024, 2048 in all within a row
- input_weight: bfloat16 [1024, 4096], replicated, may hold values from -0.1875 to 0.1875
- output_weight: bfloat16 [1024, 1024], replicated, may hold values from -0.1875 to 0.1875
- cotangent: bfloat16 [16384, 1024], P(('dp', 'cp')), may hold values from -6 to 6
Outputs:
- layer_out: bfloat16 [16384, 1024], P(('dp', 'cp'))
- table_grad: float32 [262144, 1024], P(('dp', 'cp'))
The draws below stay inside these ranges and needn't reach their ends.
Inputs may be any that keep to these rules, and one draw needn't show every extreme that they name: `owners`: among the events of one device no shard is named more than 2 times, and some device names one shard exactly 2 times. `history_lengths`: the 3 lengths of a cycle group sum to 2048; the longest is exactly 1024.
All inputs are finite; a program needn't handle non-finite values.
Results may differ from the reference program's by a relative error of at most 0.0043.
Values may be sent and summed in bfloat16 or wider, within the bound.
No kernel may reach another device: no remote copies, remote signals or barrier semaphores. Data moves between devices by JAX's collectives and lax.ppermute only.
A program may use at most 128 MiB of HBM per device.

```python
import math
import jax
import jax.numpy as jnp
import numpy as np
from jax import lax

D = 1024
HEADS = 8
HDIM = 128
TAB_DEV = 2048
NDOC = 3
ROWS = 128
SHARDS = 128
GROUPS = 8
CAP = 2
CYCLE = 2048
LMAX = 1024
TOKENS = 16384
VOCAB = 262144
N_CP = 16


def with_ends(entries, rng, least, high):
    longest = entries.shape.index(max(entries.shape))
    spots = []
    for shift in (0, 1):
        where = [jax.random.randint(jax.random.fold_in(rng, axis), (), 0, length) for axis, length in enumerate(entries.shape)]
        where[longest] = (where[longest] + shift) % entries.shape[longest]
        spots.append(tuple(where))
    return entries.at[spots[0]].set(least).at[spots[1]].set(high)


def block_levels(rng, extent, pieces, low, largest):
    def one(axis_at, parts):
        draws = jax.random.uniform(jax.random.fold_in(jax.random.fold_in(rng, 6), axis_at), (parts,), jnp.float32, low / len(pieces), largest / len(pieces))
        return jnp.repeat(jnp.exp(draws), extent[axis_at] // parts).reshape((-1,) + (1,) * (len(extent) - axis_at - 1))

    gain = one(*pieces[0])
    for cut in pieces[1:]:
        gain = gain * one(*cut)
    return gain


def split_up(amount, total, reach, slope):
    portions = [(1 << 20) // math.isqrt(grade ** slope) + 1 for grade in range(2, amount + 1)]
    surplus, holding = total - reach - (amount - 1), [1] * (amount - 1)
    while surplus > 0:
        movable = [i for i in range(amount - 1) if holding[i] < reach]
        pool, left = sum([portions[i] for i in movable]), surplus
        for i in movable:
            addition = min(reach - holding[i], max(1, left * portions[i] // pool), surplus)
            holding[i] = holding[i] + addition
            surplus = surplus - addition
    return np.array([reach] + holding)


def ragged(rng, count, total, most, lean):
    if count == 2:
        one = jax.random.randint(rng, (), max(1, total - most), min(most, total - 1) + 1)
        return jnp.stack([one, total - one])
    tallies = jnp.asarray(split_up(count, total, most, lean), jnp.int32)
    couples = (count - 1) // 2
    donor, receiver = tallies[1:1 + 2 * couples:2], tallies[2:2 + 2 * couples:2]
    margin = jnp.minimum(donor - 1, most - receiver)
    moved = jax.random.randint(jax.random.fold_in(rng, 1), (couples,), 0, 1 << 20) % (margin + 1)
    tallies = tallies.at[1:1 + 2 * couples:2].set(donor - moved).at[2:2 + 2 * couples:2].set(receiver + moved)
    return tallies[jax.random.permutation(jax.random.fold_in(rng, 2), count)]


def routed_block(key, own, number, rows, count, top, most, lean):
    ranking = jax.random.permutation(key, count)
    crowded, usual = shares(count, rows * top, most, lean, True), shares(count, rows * top, most, lean, False)
    places = jnp.arange(count)

    def named(sizes, rotation):
        used = int((sizes > 0).sum())
        fixed = max(1, used // 4)
        moved = fixed + (places - fixed + rotation * (used - fixed)) % max(1, count - fixed)
        return jnp.zeros((count,), jnp.int32).at[ranking[jnp.where(places < fixed, places, moved)]].set(jnp.asarray(sizes, jnp.int32))

    sizes = jnp.where(number % 4 == 0, named(crowded, number // 4), named(usual, number - number // 4 - 1))
    mixed = jax.random.permutation(jax.random.fold_in(own, 3), count)
    source_of, sink = mixed[0:count // 2 * 2:2], mixed[1:count // 2 * 2:2]
    room = jnp.minimum(sizes[source_of] - 1, most - sizes[sink]) // 2
    room = jnp.where((source_of == ranking[0]) | (sink == ranking[0]) | (sizes[sink] == 0), 0, jnp.maximum(room, 0))
    moved = jax.random.randint(jax.random.fold_in(own, 4), (count // 2,), 0, 1 << 20) % (room + 1)
    sizes = sizes.at[source_of].add(-moved).at[sink].add(moved)
    items = jnp.searchsorted(jnp.cumsum(sizes), jnp.arange(rows * top), side="right").astype(jnp.int32)
    table = items.reshape(top, rows).T
    table = table[jax.random.permutation(jax.random.fold_in(own, 1), rows)]
    rotation = jax.random.randint(jax.random.fold_in(own, 2), (rows, 1), 0, top)
    return jnp.take_along_axis(table, (jnp.arange(top)[None, :] + rotation) % top, axis=1)


def shares(count, total, reach, slope, full):
    weights = [(1 << 20) // math.isqrt(grade ** slope) + 1 for grade in range(1, count + 1)]
    largest = reach if full else min(reach, max(-(-total // count), total * weights[0] // sum(weights)))
    least = 1 if total - largest >= count - 1 else 0
    given, surplus = [largest] + [least] * (count - 1), total - largest - least * (count - 1)
    while surplus > 0:
        free = [i for i in range(1, count) if given[i] < largest] or [i for i in range(1, count) if given[i] < reach]
        whole, remaining = sum([weights[i] for i in free]), surplus
        for i in free:
            more = min(reach - given[i], max(1, remaining * weights[i] // whole), surplus)
            given[i] = given[i] + more
            surplus = surplus - more
    return np.array(given)


def centred(stream_key, dims, deviation, reach, cuts=(), held_as=jnp.bfloat16):
    result = deviation * jax.random.normal(stream_key, dims, jnp.float32)
    if cuts:
        result = result * block_levels(stream_key, dims, cuts, -0.22, 0.18)
    return jnp.clip(result, -reach, reach).astype(held_as)


def setup_inputs(seed: int = 0) -> dict:
    splits = jax.random.split(jax.random.key(seed), 9)
    table_rows = centred(splits[0], (VOCAB, D), 1.0, 6.0, ((0, 128),))
    row_scales = jnp.clip(jnp.exp(math.log(4.0) - 2.7725887 * jax.random.uniform(splits[1], (VOCAB,), jnp.float32) ** block_levels(splits[1], (VOCAB,), ((0, 128),), -0.2, 0.2)), 0.25, 4.0)
    owners_keys = jax.random.split(jax.random.fold_in(splits[2], 1), TOKENS // ROWS)
    owners_turns = jax.random.permutation(jax.random.fold_in(splits[2], 3), TOKENS // ROWS)
    owners = jax.vmap(lambda own, number: routed_block(jax.random.fold_in(splits[2], 2), own, number, ROWS, SHARDS, 1, CAP, 2))(owners_keys, owners_turns).reshape((TOKENS, 1))
    shard_rows = with_ends(jax.random.randint(splits[3], (TOKENS,), 0, TAB_DEV), jax.random.fold_in(splits[3], 1), 0, TAB_DEV - 1).astype(jnp.int32)
    history_lengths = jax.vmap(lambda own: ragged(own, NDOC, CYCLE, LMAX, 2))(jax.random.split(splits[4], GROUPS)).reshape((GROUPS, NDOC)).astype(jnp.int32)
    input_weight = centred(splits[5], (D, 4 * D), D ** -0.5, 0.1875)
    output_weight = centred(splits[6], (D, D), D ** -0.5, 0.1875)
    cotangent = centred(splits[7], (TOKENS, D), 1.0, 6.0, ((0, 128),))
    return dict(table_rows=table_rows, row_scales=row_scales, owners=owners, shard_rows=shard_rows, history_lengths=history_lengths, input_weight=input_weight, output_weight=output_weight, cotangent=cotangent)


EPSILON = 1e-05

def doc_bounds(lengths, positions):
    lengths = lengths.astype(jnp.int32)
    ends_at = jnp.cumsum(lengths).astype(jnp.int32)
    begins_at = ends_at - lengths
    inside = (positions[:, None] >= begins_at[None, :]) & (positions[:, None] < ends_at[None, :])
    doc_first = lax.optimization_barrier(jnp.sum(jnp.where(inside, begins_at[None, :], 0), axis=1)).astype(jnp.int32)
    doc_length = lax.optimization_barrier(jnp.sum(jnp.where(inside, lengths[None, :], 0), axis=1)).astype(jnp.float32)
    return (doc_first, doc_length)

def normalize(values):
    center = lax.optimization_barrier(jnp.mean(values, axis=-1, keepdims=True))
    shifted = values - center
    inv_spread = lax.rsqrt(lax.optimization_barrier(jnp.mean(shifted * shifted, axis=-1, keepdims=True)) + EPSILON)
    return (shifted * inv_spread, inv_spread)

def normalize_back(grad_in, normed, inv_spread):
    return inv_spread * (grad_in - lax.optimization_barrier(jnp.mean(grad_in, axis=-1, keepdims=True)) - normed * lax.optimization_barrier(jnp.mean(grad_in * normed, axis=-1, keepdims=True)))

def score_block(queries, key_block, query_pos, query_first, key_pos):
    scaling = queries.shape[-1] ** (-0.5)
    scores = jnp.einsum('qhe,khe->hqk', queries.astype(jnp.float32), key_block.astype(jnp.float32)) * scaling
    allowed = (key_pos[None, :] >= query_first[:, None]) & (key_pos[None, :] <= query_pos[:, None])
    return (scores, allowed[None])

def forward_part(queries, key_block, value_block, query_pos, query_first, query_length, key_pos):
    scores, allowed = score_block(queries, key_block, query_pos, query_first, key_pos)
    weights = jnp.where(allowed, scores * jax.nn.sigmoid(scores) / query_length[None, :, None], 0.0).astype(jnp.bfloat16)
    return jnp.einsum('hqk,khe->qhe', weights.astype(jnp.float32), value_block.astype(jnp.float32))

def backward_part(queries, key_block, value_block, grad_out, query_pos, query_first, query_length, key_pos):
    scores, allowed = score_block(queries, key_block, query_pos, query_first, key_pos)
    sigmoid_part = jax.nn.sigmoid(scores)
    weights = jnp.where(allowed, scores * sigmoid_part / query_length[None, :, None], 0.0).astype(jnp.bfloat16)
    grad_weights = jnp.einsum('qhe,khe->hqk', grad_out.astype(jnp.float32), value_block.astype(jnp.float32))
    silu_slope = sigmoid_part * (1.0 + scores * (1.0 - sigmoid_part))
    scaling = queries.shape[-1] ** (-0.5)
    grad_scores = jnp.where(allowed, grad_weights * silu_slope / query_length[None, :, None] * scaling, 0.0).astype(jnp.bfloat16)
    grad_query = jnp.einsum('hqk,khe->qhe', grad_scores.astype(jnp.float32), key_block.astype(jnp.float32))
    grad_key = jnp.einsum('hqk,qhe->khe', grad_scores.astype(jnp.float32), queries.astype(jnp.float32))
    grad_value = jnp.einsum('hqk,qhe->khe', weights.astype(jnp.float32), grad_out.astype(jnp.float32))
    return (grad_query, grad_key, grad_value)

def reference(table_rows, row_scales, owners, shard_rows, history_lengths, input_weight, output_weight, cotangent):
    item_ids = (owners[:, 0] * TAB_DEV + shard_rows).astype(jnp.int32)
    embedded = table_rows[item_ids].astype(jnp.float32) * row_scales[item_ids][:, None]

    def one_group(packed):
        group_embed, group_grad, lengths = packed
        positions = jnp.arange(CYCLE, dtype=jnp.int32)
        query_first, query_length = doc_bounds(lengths, positions)
        normed, inv_embed = normalize(group_embed)
        projected = jnp.dot(normed.astype(jnp.bfloat16), input_weight, preferred_element_type=jnp.float32)
        activated = (projected * jax.nn.sigmoid(projected)).astype(jnp.bfloat16)
        gate_rows = activated[:, :D]
        value_heads = activated[:, D:2 * D].reshape(CYCLE, HEADS, HDIM)
        query_heads = activated[:, 2 * D:3 * D].reshape(CYCLE, HEADS, HDIM)
        key_heads = activated[:, 3 * D:].reshape(CYCLE, HEADS, HDIM)

        def shard_slices(shard):
            block_start = (shard * ROWS).astype(jnp.int32)
            return (lax.dynamic_slice_in_dim(query_heads, block_start, ROWS, 0), lax.dynamic_slice_in_dim(positions, block_start, ROWS, 0), lax.dynamic_slice_in_dim(query_first, block_start, ROWS, 0), lax.dynamic_slice_in_dim(query_length, block_start, ROWS, 0), block_start)

        def shard_forward(shard):
            queries, query_pos, first_part, length_part, block_start = shard_slices(shard)
            return forward_part(queries, key_heads, value_heads, query_pos, first_part, length_part, positions)
        shards = jnp.arange(N_CP, dtype=jnp.int32)
        attention = lax.map(shard_forward, shards).reshape(CYCLE, D)
        attn_norm, inv_attn = normalize(attention)
        mixed = attn_norm * gate_rows.astype(jnp.float32)
        output = group_embed + jnp.dot(mixed.astype(jnp.bfloat16), output_weight, preferred_element_type=jnp.float32)
        layer_part = output.astype(jnp.bfloat16)
        grad_mixed = jnp.dot(group_grad, output_weight.T, preferred_element_type=jnp.float32)
        grad_gate = grad_mixed * attn_norm
        grad_attn = normalize_back(grad_mixed * gate_rows.astype(jnp.float32), attn_norm, inv_attn).astype(jnp.bfloat16)
        grad_heads = grad_attn.reshape(CYCLE, HEADS, HDIM)

        def shard_backward(running, shard):
            queries, query_pos, first_part, length_part, block_start = shard_slices(shard)
            grad_piece = lax.dynamic_slice_in_dim(grad_heads, block_start, ROWS, 0)
            grad_query, grad_key, grad_value = backward_part(queries, key_heads, value_heads, grad_piece, query_pos, first_part, length_part, positions)
            return ((running[0] + grad_key, running[1] + grad_value), grad_query)
        zeros_all = jnp.zeros((CYCLE, HEADS, HDIM), jnp.float32)
        (grad_key, grad_value), grad_query = lax.scan(shard_backward, (zeros_all, zeros_all), shards)
        grad_act = jnp.concatenate([grad_gate, grad_value.reshape(CYCLE, D), grad_query.reshape(CYCLE, D), grad_key.reshape(CYCLE, D)], axis=1)
        sigmoid_part = jax.nn.sigmoid(projected)
        grad_proj = (grad_act * sigmoid_part * (1.0 + projected * (1.0 - sigmoid_part))).astype(jnp.bfloat16)
        grad_norm = jnp.dot(grad_proj, input_weight.T, preferred_element_type=jnp.float32)
        grad_embed = group_grad.astype(jnp.float32) + normalize_back(grad_norm, normed, inv_embed)
        return (layer_part, grad_embed)
    layer_out, grad_embed = lax.map(one_group, (embedded.reshape(GROUPS, CYCLE, D), cotangent.reshape(GROUPS, CYCLE, D), history_lengths))
    layer_out = layer_out.reshape(TOKENS, D)
    grad_embed = grad_embed.reshape(TOKENS, D)
    table_grad = row_scales[:, None] * jax.ops.segment_sum(grad_embed, item_ids, num_segments=VOCAB)
    return (layer_out, table_grad)
```

```python
import jax
import jax.numpy as jnp
from jax import lax
from jax.sharding import PartitionSpec as P

HEADS = 8
EPSILON = 1e-05


def normalize(values):
    center = jnp.mean(values, axis=-1, keepdims=True)
    shifted = values - center
    inv_spread = lax.rsqrt(jnp.mean(shifted * shifted, axis=-1, keepdims=True) + EPSILON)
    return (shifted * inv_spread, inv_spread)


def normalize_back(grad_in, normed, inv_spread):
    return inv_spread * (
        grad_in
        - jnp.mean(grad_in, axis=-1, keepdims=True)
        - normed * jnp.mean(grad_in * normed, axis=-1, keepdims=True)
    )


def split_scale(scale):
    high = lax.reduce_precision(scale, 8, 7)
    rest = scale - high
    middle = lax.reduce_precision(rest, 8, 7)
    return high, middle, rest - middle


def per_device(
    table_rows,
    row_scales,
    owners,
    shard_rows,
    history_lengths,
    input_weight,
    output_weight,
    cotangent,
):
    f32, bf16 = jnp.float32, jnp.bfloat16
    rows = owners.shape[0]
    table_size, width = table_rows.shape
    heads = HEADS
    hdim = width // heads
    devices = lax.axis_size(("dp", "cp"))
    n_cp = lax.axis_size("cp")
    cores = n_cp // heads
    capacity = 2
    slots = devices * capacity
    cycle = rows * n_cp
    half = cycle // 2
    quarter = heads // 2
    groups = [[heads_i * cores + c for heads_i in range(heads)] for c in range(cores)]
    swap = [(i, i ^ 1) for i in range(n_cp)]
    core = lax.axis_index("cp") % cores

    target = owners[:, 0]
    matches = target[:, None] == jnp.arange(devices, dtype=jnp.int32)[None, :]
    counts = matches.astype(jnp.int32)
    ranked = jnp.sum((jnp.cumsum(counts, axis=0) - counts) * counts, axis=1)
    placing = matches[:, :, None] & (ranked[:, None, None] == jnp.arange(capacity, dtype=jnp.int32))
    requests = jnp.sum(jnp.where(placing, shard_rows[:, None, None] + 1, 0), axis=0)
    incoming = lax.all_to_all(
        requests, ("dp", "cp"), split_axis=0, concat_axis=0, tiled=True
    ).reshape(slots)
    place = placing.reshape(rows, slots).astype(bf16)
    chosen = (
        (incoming - 1)[:, None] == jnp.arange(table_size, dtype=jnp.int32)[None, :]
    ).astype(bf16)

    pieces = jnp.stack(split_scale(row_scales), axis=1).astype(bf16)
    pieces = jnp.pad(pieces, ((0, 0), (0, 125)))
    fetched = jnp.concatenate(
        [
            jnp.dot(chosen, table_rows, preferred_element_type=f32).astype(bf16),
            jnp.dot(chosen, pieces, preferred_element_type=f32).astype(bf16),
        ],
        axis=1,
    )
    returned = lax.all_to_all(
        fetched.reshape(devices, capacity, width + 128),
        ("dp", "cp"),
        split_axis=0,
        concat_axis=0,
        tiled=True,
    ).reshape(slots, width + 128)
    gathered = jnp.dot(place, returned, preferred_element_type=f32)
    scale = gathered[:, width] + (gathered[:, width + 1] + gathered[:, width + 2])
    embedded = gathered[:, :width] * scale[:, None]

    def to_heads(values):
        return lax.all_to_all(
            values, "cp", split_axis=0, concat_axis=0, tiled=True, axis_index_groups=groups
        )

    lengths = history_lengths[0]
    ends = jnp.cumsum(lengths)
    begins = ends - lengths
    longest = jnp.sum(jnp.where(lengths == jnp.max(lengths), begins, 0))
    residue = jnp.arange(half, dtype=jnp.int32)
    upper = (residue >= longest) ^ (core == 1)
    position = jnp.where(upper, residue, residue + half)
    inside = (position[:, None] >= begins[None, :]) & (position[:, None] < ends[None, :])
    first = jnp.sum(jnp.where(inside, begins[None, :], 0), axis=1)
    length = jnp.sum(jnp.where(inside, lengths[None, :], 0), axis=1).astype(f32)
    own = (
        jnp.arange(quarter, dtype=jnp.int32)[:, None] * (2 * rows)
        + core * rows
        + jnp.arange(rows, dtype=jnp.int32)[None, :]
    )
    own_upper = ((own >= longest) ^ (core == 1))[:, :, None]

    def split_histories(values):
        keep = jnp.where(own_upper, values[:quarter], values[quarter:])
        send = jnp.where(own_upper, values[quarter:], values[:quarter])
        received = lax.ppermute(send, "cp", swap)
        pair = jnp.where(
            core == 0, jnp.stack([keep, received], 1), jnp.stack([received, keep], 1)
        )
        return pair.reshape(half, values.shape[-1])

    def join_histories(values):
        pair = values.reshape(quarter, 2, rows, values.shape[-1])
        keep = jnp.where(core == 0, pair[:, 0], pair[:, 1])
        send = jnp.where(core == 0, pair[:, 1], pair[:, 0])
        received = lax.ppermute(send, "cp", swap)
        return jnp.concatenate(
            [jnp.where(own_upper, keep, received), jnp.where(own_upper, received, keep)], axis=0
        )

    grad_mixed = jnp.einsum("rk,dk->rd", cotangent, output_weight, preferred_element_type=f32)
    grad_mixed_heads = split_histories(
        to_heads(grad_mixed.astype(bf16).reshape(rows, heads, hdim).transpose(1, 0, 2))
    )

    normed, inv_embed = normalize(embedded)
    projected = jnp.dot(normed.astype(bf16), input_weight, preferred_element_type=f32)
    activated = (projected * jax.nn.sigmoid(projected)).astype(bf16)
    branches = to_heads(
        activated.reshape(rows, 4, heads, hdim).transpose(2, 0, 1, 3).reshape(heads, rows, 4 * hdim)
    )
    branches = split_histories(branches)
    gate, value, query, key = [branches[:, i * hdim : (i + 1) * hdim] for i in range(4)]

    scaling = hdim ** (-0.5)
    scores = jnp.einsum("qe,ke->qk", query, key, preferred_element_type=f32) * scaling
    allowed = (position[None, :] >= first[:, None]) & (position[None, :] <= position[:, None])
    sig = jax.nn.sigmoid(scores)
    weights = jnp.where(allowed, scores * sig / length[:, None], 0.0).astype(bf16)
    slope = jnp.where(
        allowed, sig * (1.0 + scores * (1.0 - sig)) / length[:, None] * scaling, 0.0
    )
    attention = jnp.dot(weights, value, preferred_element_type=f32)

    gated = grad_mixed_heads.astype(f32) * gate.astype(f32)
    center = jnp.mean(attention, axis=1)
    shifted = attention - center[:, None]
    stats = jnp.stack(
        [
            center,
            jnp.sum(shifted * shifted, axis=1),
            jnp.sum(gated, axis=1),
            jnp.sum(gated * shifted, axis=1),
        ]
    )
    stats = to_heads(jnp.broadcast_to(stats[None], (heads,) + stats.shape))
    mean = jnp.mean(stats[:, 0], axis=0)
    offset = stats[:, 0] - mean[None]
    variance = jnp.sum(stats[:, 1] + hdim * offset * offset, axis=0) / width
    inv_attn = lax.rsqrt(variance + EPSILON)
    mean_grad = jnp.sum(stats[:, 2], axis=0) / width
    mean_prod = inv_attn * jnp.sum(stats[:, 3] + offset * stats[:, 2], axis=0) / width
    attn_norm = (attention - mean[:, None]) * inv_attn[:, None]
    grad_attn = (
        inv_attn[:, None] * (gated - mean_grad[:, None] - attn_norm * mean_prod[:, None])
    ).astype(bf16)

    grad_weights = jnp.einsum("qe,ke->qk", grad_attn, value, preferred_element_type=f32)
    grad_scores = (grad_weights * slope).astype(bf16)
    grad_query = jnp.dot(grad_scores, key, preferred_element_type=f32)
    grad_key = jnp.einsum("qk,qe->ke", grad_scores, query, preferred_element_type=f32)
    grad_value = jnp.einsum("qk,qe->ke", weights, grad_attn, preferred_element_type=f32)

    back = jnp.concatenate([attn_norm, grad_value, grad_query, grad_key], axis=1).astype(bf16)
    back = to_heads(join_histories(back))
    back = back.reshape(heads, rows, 4, hdim).transpose(1, 2, 0, 3).reshape(rows, 4, width)
    attn_norm_rows = back[:, 0].astype(f32)
    mixed = attn_norm_rows * activated[:, :width].astype(f32)
    layer_out = (
        embedded + jnp.dot(mixed.astype(bf16), output_weight, preferred_element_type=f32)
    ).astype(bf16)
    grad_act = jnp.concatenate(
        [grad_mixed * attn_norm_rows, back[:, 1:].reshape(rows, 3 * width).astype(f32)], axis=1
    )
    sig = jax.nn.sigmoid(projected)
    grad_proj = (grad_act * sig * (1.0 + projected * (1.0 - sig))).astype(bf16)
    grad_norm = jnp.einsum("rk,dk->rd", grad_proj, input_weight, preferred_element_type=f32)
    grad_embed = cotangent.astype(f32) + normalize_back(grad_norm, normed, inv_embed)

    outgoing = jnp.einsum(
        "rs,rd->sd", place, grad_embed.astype(bf16), preferred_element_type=f32
    ).astype(bf16)
    arrived = lax.all_to_all(
        outgoing.reshape(devices, capacity, width),
        ("dp", "cp"),
        split_axis=0,
        concat_axis=0,
        tiled=True,
    ).reshape(slots, width)
    table_grad = (
        jnp.einsum("sr,sd->rd", chosen, arrived, preferred_element_type=f32) * row_scales[:, None]
    )
    return (layer_out, table_grad)


def solution(mesh):
    return jax.shard_map(
        per_device,
        mesh=mesh,
        in_specs=(
            P(("dp", "cp"), None),
            P(("dp", "cp")),
            P(("dp", "cp"), None),
            P(("dp", "cp")),
            P("dp", None),
            P(),
            P(),
            P(("dp", "cp"), None),
        ),
        out_specs=(P(("dp", "cp"), None), P(("dp", "cp"), None)),
        check_vma=False,
    )
```

```python
import jax
import jax.numpy as jnp
from jax import lax
from jax.experimental import pallas as pl
from jax.experimental.pallas import tpu as pltpu
from jax.sharding import PartitionSpec as P

HEADS = 8
EPSILON = 1e-05
CAPACITY = 2
TILE = 256
F32, BF16, I32 = jnp.float32, jnp.bfloat16, jnp.int32


def nt_dot(left, right):
    return lax.dot_general(left, right, (((1,), (1,)), ((), ())), preferred_element_type=F32)


def tn_dot(left, right):
    return lax.dot_general(left, right, (((0,), (0,)), ((), ())), preferred_element_type=F32)


def nn_dot(left, right):
    return jnp.dot(left, right, preferred_element_type=F32)


def iota(shape, axis):
    return lax.broadcasted_iota(I32, shape, axis)


def normalize(values):
    center = jnp.mean(values, axis=-1, keepdims=True)
    shifted = values - center
    inv_spread = lax.rsqrt(jnp.mean(shifted * shifted, axis=-1, keepdims=True) + EPSILON)
    return (shifted * inv_spread, inv_spread)


def normalize_back(grad_in, normed, inv_spread):
    return inv_spread * (
        grad_in
        - jnp.mean(grad_in, axis=-1, keepdims=True)
        - normed * jnp.mean(grad_in * normed, axis=-1, keepdims=True)
    )


def full(shape):
    return pl.BlockSpec(shape, lambda *_: (0,) * len(shape))


def params(steps=0):
    if steps:
        return pltpu.CompilerParams(dimension_semantics=("arbitrary",))
    return pltpu.CompilerParams()


def request_kernel(core_ref, lengths_ref, owner_ref, row_ref, request_ref, slot_ref, facts_ref):
    shape = request_ref.shape
    match = owner_ref[...] == iota(shape, 0)
    earlier = jnp.where(iota(shape, 0) < iota(shape, 1), 1.0, 0.0).astype(BF16)
    before = nn_dot(jnp.where(match, 1.0, 0.0).astype(BF16), earlier)
    rank = jnp.sum(jnp.where(match, before, 0.0), axis=0, keepdims=True).astype(I32)
    slot_ref[...] = owner_ref[...] * CAPACITY + rank
    wanted = row_ref[...].astype(F32) + 1.0
    lists = [
        jnp.sum(jnp.where(match & (before == c), wanted, 0.0), axis=1, keepdims=True)
        for c in range(CAPACITY)
    ]
    lane = iota(shape, 1)
    request_ref[...] = jnp.where(
        lane == 0, lists[0], jnp.where(lane == 1, lists[1], 0.0)
    ).astype(I32)
    core = core_ref[0]
    one, two, three = lengths_ref[0, 0], lengths_ref[0, 1], lengths_ref[0, 2]
    half = (one + two + three) // 2
    most = jnp.maximum(one, jnp.maximum(two, three))
    longest = jnp.where(one == most, 0, jnp.where(two == most, one, one + two))
    inner = jnp.where(one == most, two, one)
    facts_ref[0] = core
    facts_ref[1] = jnp.where(core == 0, longest & (half - 1), 0)
    facts_ref[2] = jnp.where(core == 0, 0, inner)
    facts_ref[3] = longest


def split_scale(scale):
    high = scale.astype(BF16).astype(F32)
    rest = scale - high
    middle = rest.astype(BF16).astype(F32)
    return high, middle, rest - middle


def fetch_kernel(incoming_ref, table_ref, scale_ref, out_ref, chosen_ref):
    step = pl.program_id(0)
    slots, size = chosen_ref.shape
    chunk = table_ref.shape[1]
    width = chunk * pl.num_programs(0)

    @pl.when(step == 0)
    def _():
        devices = slots // CAPACITY
        device_of = iota((slots, devices), 0) >> 1 == iota((slots, devices), 1)
        spread = jnp.where(device_of, 1.0, 0.0).astype(BF16)
        wanted = incoming_ref[...]
        high = nn_dot(spread, (wanted >> 4).astype(F32).astype(BF16))
        low = nn_dot(spread, (wanted & 15).astype(F32).astype(BF16))
        mine = iota((slots, 128), 1) == (iota((slots, 128), 0) & 1)
        row = jnp.sum(jnp.where(mine, high * 16.0 + low, 0.0), axis=1, keepdims=True)
        chosen = row.astype(I32) - 1 == iota((slots, size), 1)
        chosen_ref[...] = jnp.where(chosen, 1.0, 0.0).astype(BF16)
        scale = jnp.sum(jnp.where(chosen, scale_ref[...], 0.0), axis=1, keepdims=True)
        high, middle, low = split_scale(scale)
        lane = iota((slots, 128), 1)
        pieces = jnp.where(
            lane == 0, high, jnp.where(lane == 1, middle, jnp.where(lane == 2, low, 0.0))
        )
        out_ref[:, 1024:1152] = pieces.astype(BF16)

    base = pl.multiple_of(step * chunk, chunk)
    out_ref[:, pl.ds(base, chunk)] = nn_dot(chosen_ref[...], table_ref[...]).astype(BF16)


def project_kernel(gathered_ref, mixed_ref, wu, wv, wq, wk, packed_ref, proj_ref, embed_ref, norm):
    width = embed_ref.shape[1]

    @pl.when(pl.program_id(0) == 0)
    def _():
        total = gathered_ref[...]
        scale = total[:, width : width + 1] + (
            total[:, width + 1 : width + 2] + total[:, width + 2 : width + 3]
        )
        embedded = total[:, :width] * scale
        embed_ref[...] = embedded
        norm[...] = normalize(embedded)[0].astype(BF16)

    for t, w in enumerate((wu, wv, wq, wk)):
        projected = nn_dot(norm[...], w[...])
        proj_ref[t] = projected
        active = (projected * jax.nn.sigmoid(projected)).astype(BF16)
        for i in range(2):
            packed_ref[i, :, t * 128 : (t + 1) * 128] = active[:, i * 128 : (i + 1) * 128]
    for i in range(2):
        packed_ref[i, :, 512:640] = mixed_ref[:, i * 128 : (i + 1) * 128].astype(BF16)


def upper_rows(facts, s, shape):
    rows = shape[0]
    residue = s * 2 * rows + facts[0] * rows + iota(shape, 0)
    return (jnp.where(residue >= facts[3], 1, 0) ^ facts[0]) == 1


def choose(mask, yes, no):
    return jnp.where(mask, yes.astype(F32), no.astype(F32)).astype(BF16)


def split_kernel(facts, x_ref, send_ref):
    quarter = send_ref.shape[0]
    for s in range(quarter):
        upper = upper_rows(facts, s, send_ref.shape[1:])
        send_ref[s] = choose(upper, x_ref[s + quarter], x_ref[s])


def join_kernel(facts, mine_ref, received_ref, out_ref):
    quarter = mine_ref.shape[0]
    for s in range(quarter):
        upper = upper_rows(facts, s, mine_ref.shape[1:])
        out_ref[s] = choose(upper, mine_ref[s], received_ref[s])
        out_ref[s + quarter] = choose(upper, received_ref[s], mine_ref[s])


def needed_keys(block, count):
    return list(range(count)) if block == 0 else list(range(block + 1))


def block_base(block, shift, count):
    return pl.multiple_of(((shift // TILE + block) & (count - 1)) * TILE, TILE)


def order_of(base, shape, axis, shift, half):
    return (base + iota(shape, axis) - shift) & (half - 1)


def query_terms(place, bound, half):
    later = place >= bound
    length = jnp.where(later, half - bound, bound).astype(F32)
    return jnp.where(later, bound, 0), 1.0 / length


def attend_kernel(facts, x_ref, received_ref, y_ref, att_ref, stats_ref):
    core, shift, bound = facts[0], facts[1], facts[2]
    half = y_ref.shape[0]
    quarter, rows, lanes = received_ref.shape
    heads = stats_ref.shape[0]
    for s in range(quarter):
        keep = choose(upper_rows(facts, s, (rows, lanes)), x_ref[s], x_ref[s + quarter])
        near = pl.multiple_of((2 * s + core) * rows, rows)
        far = pl.multiple_of((2 * s + 1 - core) * rows, rows)
        y_ref[pl.ds(near, rows), :] = keep
        y_ref[pl.ds(far, rows), :] = received_ref[s]

    hdim = 128
    scaling = hdim ** (-0.5)
    count = half // TILE
    for qi in range(count):
        base = block_base(qi, shift, count)
        span = pl.ds(base, TILE)
        place = order_of(base, (TILE, 1), 0, shift, half)
        first, inv_length = query_terms(place, bound, half)
        query = y_ref[span, 256:384]
        attention = 0.0
        for ki in needed_keys(qi, count):
            key_base = block_base(ki, shift, count)
            keys = pl.ds(key_base, TILE)
            scores = nt_dot(query, y_ref[keys, 384:512]) * scaling
            at = order_of(key_base, (1, TILE), 1, shift, half)
            allowed = (at <= place) & (at >= first)
            weights = jnp.where(
                allowed, scores * jax.nn.sigmoid(scores) * inv_length, 0.0
            ).astype(BF16)
            attention += nn_dot(weights, y_ref[keys, 128:256])

        att_ref[span, :] = attention
        gated = y_ref[span, 512:640].astype(F32) * y_ref[span, 0:128].astype(F32)
        center = jnp.mean(attention, axis=1, keepdims=True)
        shifted = attention - center
        columns = [
            center,
            jnp.sum(shifted * shifted, axis=1, keepdims=True),
            jnp.sum(gated, axis=1, keepdims=True),
            jnp.sum(gated * shifted, axis=1, keepdims=True),
        ]
        lane = iota((TILE, 128), 1)
        table = jnp.zeros((TILE, 128), F32)
        for i, column in enumerate(columns):
            table = jnp.where(lane == i, column, table)
        turned = table.T[0:4]
        for h in range(heads):
            stats_ref[h, :, span] = turned


def backward_kernel(facts, y_ref, att_ref, stats_ref, mine_ref, send_ref, attn, grad, dq, dk, dv):
    core, shift, bound = facts[0], facts[1], facts[2]
    half = y_ref.shape[0]
    heads = stats_ref.shape[0]
    quarter, rows = mine_ref.shape[0], mine_ref.shape[1]
    hdim = 128
    width = heads * hdim
    scaling = hdim ** (-0.5)
    count = half // TILE
    stat = [[stats_ref[h, i : i + 1, :] for i in range(4)] for h in range(heads)]
    mean = sum(s[0] for s in stat) / heads
    variance, mean_grad, mean_prod = 0.0, 0.0, 0.0
    for center, spread, grad_sum, prod_sum in stat:
        offset = center - mean
        variance += spread + hdim * offset * offset
        mean_grad += grad_sum
        mean_prod += prod_sum + offset * grad_sum
    inv_attn = lax.rsqrt(variance / width + EPSILON)
    line = iota((128, half), 0)
    table = jnp.where(
        line == 0,
        mean,
        jnp.where(
            line == 1,
            inv_attn,
            jnp.where(line == 2, mean_grad / width, inv_attn * mean_prod / width),
        ),
    )
    columns = table.T
    for qi in range(count):
        span = slice(qi * TILE, (qi + 1) * TILE)
        inv = columns[span, 1:2]
        attn_norm = (att_ref[span, :] - columns[span, 0:1]) * inv
        gated = y_ref[span, 512:640].astype(F32) * y_ref[span, 0:128].astype(F32)
        attn[span, :] = attn_norm.astype(BF16)
        grad[span, :] = (
            inv * (gated - columns[span, 2:3] - attn_norm * columns[span, 3:4])
        ).astype(BF16)
    dq[...] = jnp.zeros_like(dq)
    for ki in range(count):
        key_base = block_base(ki, shift, count)
        keys = pl.ds(key_base, TILE)
        at = order_of(key_base, (TILE, 1), 0, shift, half)
        key, value = y_ref[keys, 384:512], y_ref[keys, 128:256]
        grad_key, grad_value = 0.0, 0.0
        for qi in range(count):
            if ki not in needed_keys(qi, count):
                continue
            base = block_base(qi, shift, count)
            span = pl.ds(base, TILE)
            place = order_of(base, (1, TILE), 1, shift, half)
            first, inv_length = query_terms(place, bound, half)
            query, grad_out = y_ref[span, 256:384], grad[span, :]
            scores = nt_dot(key, query) * scaling
            allowed = (at <= place) & (at >= first)
            sig = jax.nn.sigmoid(scores)
            product = scores * sig
            weights = jnp.where(allowed, product * inv_length, 0.0).astype(BF16)
            slope = (sig + product * (1.0 - sig)) * (inv_length * scaling)
            grad_weights = nt_dot(value, grad_out)
            grad_scores = jnp.where(allowed, grad_weights * slope, 0.0).astype(BF16)
            grad_value += nn_dot(weights, grad_out)
            grad_key += nn_dot(grad_scores, query)
            dq[span, :] += tn_dot(grad_scores, key)
        dk[keys, :] = grad_key.astype(BF16)
        dv[keys, :] = grad_value.astype(BF16)

    for s in range(quarter):
        near = pl.ds(pl.multiple_of((2 * s + core) * rows, rows), rows)
        far = pl.ds(pl.multiple_of((2 * s + 1 - core) * rows, rows), rows)
        for i, ref in enumerate((attn, dv, dq, dk)):
            columns = slice(i * hdim, (i + 1) * hdim)
            mine_ref[s, :, columns] = ref[near, :].astype(BF16)
            send_ref[s, :, columns] = ref[far, :].astype(BF16)


def finish_kernel(
    back_ref, proj_ref, mixed_ref, slot_ref, embed_ref, cot_ref, wu, wv, wq, wk, out_ref, gated_ref, acc
):
    step = pl.program_id(0)

    def part(i):
        columns = slice(i * 128, (i + 1) * 128)
        return jnp.concatenate([back_ref[0, :, columns], back_ref[1, :, columns]], axis=1).astype(F32)

    attn_norm = part(0)
    total = 0.0
    for t, w in enumerate((wu, wv, wq, wk)):
        projected = proj_ref[t]
        sig = jax.nn.sigmoid(projected)
        slope = sig * (1.0 + projected * (1.0 - sig))
        if t == 0:
            grad_act = mixed_ref[...] * attn_norm
            gate = (projected * sig).astype(BF16).astype(F32)
            gated_ref[...] = (attn_norm * gate).astype(BF16)
        else:
            grad_act = part(t)
        total += nt_dot((grad_act * slope).astype(BF16), w[...])

    @pl.when(step == 0)
    def _():
        acc[...] = total

    @pl.when(step > 0)
    def _():
        acc[...] += total

    @pl.when(step == pl.num_programs(0) - 1)
    def _():
        normed, inv_embed = normalize(embed_ref[...])
        grad_embed = cot_ref[...].astype(F32) + normalize_back(acc[...], normed, inv_embed)
        slots, rows = out_ref.shape[0], slot_ref.shape[1]
        place = jnp.where(slot_ref[...] == iota((slots, rows), 0), 1.0, 0.0).astype(BF16)
        out_ref[...] = nn_dot(place, grad_embed.astype(BF16)).astype(BF16)


def table_kernel(incoming_ref, arrived_ref, scale_ref, out_ref):
    block, slots = out_ref.shape[0], arrived_ref.shape[0]
    base = pl.program_id(0) * block
    chosen = incoming_ref[...] - 1 - base == iota((block, slots), 0)
    total = nn_dot(jnp.where(chosen, 1.0, 0.0).astype(BF16), arrived_ref[...])
    scale = jnp.broadcast_to(scale_ref[...], (128, block)).T
    out_ref[...] = total * scale[:, 0:1]


def per_device(
    table_rows,
    row_scales,
    owners,
    shard_rows,
    history_lengths,
    input_weight,
    output_weight,
    cotangent,
):
    rows = owners.shape[0]
    table_size, width = table_rows.shape
    heads = HEADS
    hdim = width // heads
    devices = lax.axis_size(("dp", "cp"))
    n_cp = lax.axis_size("cp")
    cores = n_cp // heads
    half = rows * n_cp // 2
    quarter = heads // 2
    slots = devices * CAPACITY
    groups = [[i * cores + c for i in range(heads)] for c in range(cores)]
    swap = [(i, i ^ 1) for i in range(n_cp)]
    core = (lax.axis_index("cp") % cores).reshape(1)
    everyone = ("dp", "cp")
    shape = jax.ShapeDtypeStruct
    smem = pl.BlockSpec(memory_space=pltpu.SMEM)

    def exchange(values, axes, **options):
        return lax.all_to_all(values, axes, split_axis=0, concat_axis=0, tiled=True, **options)

    def to_heads(values):
        return exchange(values, "cp", axis_index_groups=groups)

    def to_all(values):
        lanes = values.shape[1]
        return exchange(values.reshape(devices, CAPACITY, lanes), everyone).reshape(slots, lanes)

    scale_line = row_scales.reshape(1, table_size)
    requests, slot_line, facts = pl.pallas_call(
        request_kernel,
        in_specs=[smem, smem, full((1, rows)), full((1, rows))],
        out_specs=(full((devices, 128)), full((1, rows)), smem),
        out_shape=(shape((devices, 128), I32), shape((1, rows), I32), shape((4,), I32)),
        grid=(1,),
        compiler_params=params(1),
        name="request",
    )(core, history_lengths, owners.reshape(1, rows), shard_rows.reshape(1, rows))
    incoming = exchange(requests.reshape(devices, 1, 128), everyone).reshape(devices, 128)

    wide = width + 128
    chunk = width // 4
    fetched = pl.pallas_call(
        fetch_kernel,
        grid=(width // chunk,),
        in_specs=[
            full((devices, 128)),
            pl.BlockSpec((table_size, chunk), lambda i: (0, i)),
            full((1, table_size)),
        ],
        out_specs=full((slots, wide)),
        out_shape=shape((slots, wide), BF16),
        scratch_shapes=[pltpu.VMEM((slots, table_size), BF16)],
        compiler_params=params(1),
        name="fetch",
    )(incoming, table_rows, scale_line)
    returned = to_all(fetched)
    place = (slot_line == jnp.arange(slots, dtype=I32)[:, None]).astype(BF16)
    gathered = jnp.einsum("sr,sd->rd", place, returned, preferred_element_type=F32)

    grad_mixed = jnp.einsum("rk,dk->rd", cotangent, output_weight, preferred_element_type=F32)

    pair = 2 * hdim
    weight_specs = [
        pl.BlockSpec((width, pair), lambda i, t=t: (0, t * (heads // 2) + i)) for t in range(4)
    ]
    packed, projected, embedded = pl.pallas_call(
        project_kernel,
        grid=(heads // 2,),
        in_specs=[full((rows, wide)), pl.BlockSpec((rows, pair), lambda i: (0, i))] + weight_specs,
        out_specs=(
            pl.BlockSpec((2, rows, 5 * hdim), lambda i: (i, 0, 0)),
            pl.BlockSpec((4, rows, pair), lambda i: (0, 0, i)),
            full((rows, width)),
        ),
        out_shape=(
            shape((heads, rows, 5 * hdim), BF16),
            shape((4, rows, width), F32),
            shape((rows, width), F32),
        ),
        scratch_shapes=[pltpu.VMEM((rows, width), BF16)],
        compiler_params=params(1),
        name="project",
    )(gathered, grad_mixed, *([input_weight] * 4))

    branches = to_heads(packed)
    send = pl.pallas_call(
        split_kernel,
        in_specs=[smem, full(branches.shape)],
        out_specs=full((quarter, rows, 5 * hdim)),
        out_shape=shape((quarter, rows, 5 * hdim), BF16),
        grid=(1,),
        compiler_params=params(1),
        name="split",
    )(facts, branches)
    received = lax.ppermute(send, "cp", swap)
    ordered, attention, stats = pl.pallas_call(
        attend_kernel,
        in_specs=[smem, full(branches.shape), full(received.shape)],
        out_specs=(full((half, 5 * hdim)), full((half, hdim)), full((heads, 4, half))),
        out_shape=(
            shape((half, 5 * hdim), BF16),
            shape((half, hdim), F32),
            shape((heads, 4, half), F32),
        ),
        grid=(1,),
        compiler_params=params(1),
        name="attend",
    )(facts, branches, received)
    stats = to_heads(stats)

    backed = shape((quarter, rows, 4 * hdim), BF16)
    mine, send = pl.pallas_call(
        backward_kernel,
        in_specs=[smem, full(ordered.shape), full(attention.shape), full(stats.shape)],
        out_specs=(full(backed.shape), full(backed.shape)),
        out_shape=(backed, backed),
        scratch_shapes=[
            pltpu.VMEM((half, hdim), BF16),
            pltpu.VMEM((half, hdim), BF16),
            pltpu.VMEM((half, hdim), F32),
            pltpu.VMEM((half, hdim), BF16),
            pltpu.VMEM((half, hdim), BF16),
        ],
        grid=(1,),
        compiler_params=params(1),
        name="backward",
    )(facts, ordered, attention, stats)
    received = lax.ppermute(send, "cp", swap)
    joined = pl.pallas_call(
        join_kernel,
        in_specs=[smem, full(backed.shape), full(backed.shape)],
        out_specs=full((heads, rows, 4 * hdim)),
        out_shape=shape((heads, rows, 4 * hdim), BF16),
        grid=(1,),
        compiler_params=params(1),
        name="join",
    )(facts, mine, received)
    back = to_heads(joined)

    outgoing, mixed = pl.pallas_call(
        finish_kernel,
        grid=(heads // 2,),
        in_specs=[
            pl.BlockSpec((2, rows, 4 * hdim), lambda i: (i, 0, 0)),
            pl.BlockSpec((4, rows, pair), lambda i: (0, 0, i)),
            pl.BlockSpec((rows, pair), lambda i: (0, i)),
            full((1, rows)),
            full((rows, width)),
            full((rows, width)),
        ]
        + weight_specs,
        out_specs=(full((slots, width)), pl.BlockSpec((rows, pair), lambda i: (0, i))),
        out_shape=(shape((slots, width), BF16), shape((rows, width), BF16)),
        scratch_shapes=[pltpu.VMEM((rows, width), F32)],
        compiler_params=params(1),
        name="finish",
    )(back, projected, grad_mixed, slot_line, embedded, cotangent, *([input_weight] * 4))
    arrived = to_all(outgoing)
    layer_out = (
        embedded + jnp.dot(mixed, output_weight, preferred_element_type=F32)
    ).astype(BF16)

    block = 256
    table_grad = pl.pallas_call(
        table_kernel,
        grid=(table_size // block,),
        in_specs=[
            full((1, slots)),
            full((slots, width)),
            pl.BlockSpec((1, block), lambda i: (0, i)),
        ],
        out_specs=pl.BlockSpec((block, width), lambda i: (i, 0)),
        out_shape=shape((table_size, width), F32),
        compiler_params=params(1),
        name="table",
    )(incoming[:, :CAPACITY].reshape(1, slots), arrived, scale_line)
    return (layer_out, table_grad)


def solution(mesh):
    return jax.shard_map(
        per_device,
        mesh=mesh,
        in_specs=(
            P(("dp", "cp"), None),
            P(("dp", "cp")),
            P(("dp", "cp"), None),
            P(("dp", "cp")),
            P("dp", None),
            P(),
            P(),
            P(("dp", "cp"), None),
        ),
        out_specs=(P(("dp", "cp"), None), P(("dp", "cp"), None)),
        check_vma=False,
    )
```

```python
import jax
import jax.numpy as jnp
from jax import lax
from jax.experimental import pallas as pl
from jax.experimental.pallas import tpu as pltpu
from jax.sharding import PartitionSpec as P

HEADS = 8
EPSILON = 1e-05
CAPACITY = 2
TILE = 256
F32, BF16, I32 = jnp.float32, jnp.bfloat16, jnp.int32


def nt_dot(left, right):
    return lax.dot_general(left, right, (((1,), (1,)), ((), ())), preferred_element_type=F32)


def tn_dot(left, right):
    return lax.dot_general(left, right, (((0,), (0,)), ((), ())), preferred_element_type=F32)


def nn_dot(left, right):
    return jnp.dot(left, right, preferred_element_type=F32)


def copies(source, target, sems, spans):
    started = [
        pltpu.make_async_copy(source.at[span], target.at[span], sems.at[n])
        for n, span in enumerate(spans)
    ]
    for copy in started:
        copy.start()
    return started


def column_spans(total, step):
    return [(slice(None), slice(base, base + step)) for base in range(0, total, step)]


def iota(shape, axis):
    return lax.broadcasted_iota(I32, shape, axis)


def normalize(values):
    center = jnp.mean(values, axis=-1, keepdims=True)
    shifted = values - center
    inv_spread = lax.rsqrt(jnp.mean(shifted * shifted, axis=-1, keepdims=True) + EPSILON)
    return (shifted * inv_spread, inv_spread)


def normalize_back(grad_in, normed, inv_spread):
    return inv_spread * (
        grad_in
        - jnp.mean(grad_in, axis=-1, keepdims=True)
        - normed * jnp.mean(grad_in * normed, axis=-1, keepdims=True)
    )


def request_kernel(core_ref, lengths_ref, owner_ref, row_ref, request_ref, slot_ref, facts_ref):
    shape = request_ref.shape
    match = owner_ref[...] == iota(shape, 0)
    earlier = jnp.where(iota(shape, 0) < iota(shape, 1), 1.0, 0.0).astype(BF16)
    before = nn_dot(jnp.where(match, 1.0, 0.0).astype(BF16), earlier)
    rank = jnp.sum(jnp.where(match, before, 0.0), axis=0, keepdims=True).astype(I32)
    slot_ref[...] = owner_ref[...] * CAPACITY + rank
    wanted = row_ref[...].astype(F32) + 1.0
    lists = [
        jnp.sum(jnp.where(match & (before == c), wanted, 0.0), axis=1, keepdims=True)
        for c in range(CAPACITY)
    ]
    lane = iota(shape, 1)
    request_ref[...] = jnp.where(
        lane == 0, lists[0], jnp.where(lane == 1, lists[1], 0.0)
    ).astype(I32)
    core = core_ref[0]
    one, two, three = lengths_ref[0, 0], lengths_ref[0, 1], lengths_ref[0, 2]
    half = (one + two + three) // 2
    most = jnp.maximum(one, jnp.maximum(two, three))
    longest = jnp.where(one == most, 0, jnp.where(two == most, one, one + two))
    inner = jnp.where(one == most, two, one)
    facts_ref[0] = core
    facts_ref[1] = jnp.where(core == 0, longest & (half - 1), 0)
    facts_ref[2] = jnp.where(core == 0, 0, inner)
    facts_ref[3] = longest


def split_scale(scale):
    high = scale.astype(BF16).astype(F32)
    rest = scale - high
    middle = rest.astype(BF16).astype(F32)
    return high, middle, rest - middle


def fetch_kernel(incoming_ref, table_hbm, scale_ref, out_ref, table_ref, sems):
    loads = copies(table_hbm, table_ref, sems, column_spans(table_ref.shape[1], 512))
    slots, size, width = out_ref.shape[0], table_ref.shape[0], table_ref.shape[1]
    devices = slots // CAPACITY
    device_of = iota((slots, devices), 0) >> 1 == iota((slots, devices), 1)
    spread = jnp.where(device_of, 1.0, 0.0).astype(BF16)
    wanted = incoming_ref[...]
    high = nn_dot(spread, (wanted >> 4).astype(F32).astype(BF16))
    low = nn_dot(spread, (wanted & 15).astype(F32).astype(BF16))
    mine = iota((slots, 128), 1) == (iota((slots, 128), 0) & 1)
    row = jnp.sum(jnp.where(mine, high * 16.0 + low, 0.0), axis=1, keepdims=True)
    chosen = row.astype(I32) - 1 == iota((slots, size), 1)
    hot = jnp.where(chosen, 1.0, 0.0).astype(BF16)
    scale = jnp.sum(jnp.where(chosen, scale_ref[...], 0.0), axis=1, keepdims=True)
    high, middle, low = split_scale(scale)
    lane = iota((slots, 128), 1)
    pieces = jnp.where(
        lane == 0, high, jnp.where(lane == 1, middle, jnp.where(lane == 2, low, 0.0))
    )
    out_ref[:, width : width + 128] = pieces.astype(BF16)
    for n, base in enumerate(range(0, width, 512)):
        loads[n].wait()
        out_ref[:, base : base + 512] = nn_dot(hot, table_ref[:, base : base + 512]).astype(BF16)


def project_kernel(
    returned_ref, slot_ref, mixed_ref, weight_hbm, packed_ref, proj_ref, embed_ref, gate_ref, weight_ref, sems
):
    width = embed_ref.shape[1]
    loads = copies(weight_hbm, weight_ref, sems, column_spans(4 * width, width))
    heads = packed_ref.shape[0]
    slots, rows = returned_ref.shape[0], slot_ref.shape[1]
    place = jnp.where(slot_ref[...] == iota((slots, rows), 0), 1.0, 0.0).astype(BF16)
    total = tn_dot(place, returned_ref[...])
    scale = total[:, width : width + 1] + (
        total[:, width + 1 : width + 2] + total[:, width + 2 : width + 3]
    )
    embedded = total[:, :width] * scale
    embed_ref[...] = embedded
    normed = normalize(embedded)[0].astype(BF16)
    for t in range(4):
        loads[t].wait()
        for pair in range(heads // 2):
            columns = slice(pair * 256, (pair + 1) * 256)
            base = t * width + pair * 256
            projected = nn_dot(normed, weight_ref[:, base : base + 256])
            proj_ref[:, base : base + 256] = projected
            active = (projected * jax.nn.sigmoid(projected)).astype(BF16)
            if t == 0:
                gate_ref[:, columns] = active
                active = (active.astype(F32) * mixed_ref[:, columns]).astype(BF16)
            for i in range(2):
                packed_ref[2 * pair + i, :, t * 128 : (t + 1) * 128] = active[
                    :, i * 128 : (i + 1) * 128
                ]


def upper_rows(facts, core, s, shape):
    rows = shape[0]
    residue = s * 2 * rows + core * rows + iota(shape, 0)
    return (jnp.where(residue >= facts[3], 1, 0) ^ facts[0]) == 1


def choose(mask, yes, no):
    return jnp.where(mask, yes.astype(F32), no.astype(F32)).astype(BF16)


def join_kernel(facts, mine_ref, received_ref, out_ref):
    quarter = mine_ref.shape[0]
    for s in range(quarter):
        upper = upper_rows(facts, facts[0], s, mine_ref.shape[1:])
        out_ref[s] = choose(upper, mine_ref[s], received_ref[s])
        out_ref[s + quarter] = choose(upper, received_ref[s], mine_ref[s])


def needed_keys(block, count):
    return list(range(count)) if block == 0 else list(range(block + 1))


def block_base(block, shift, count):
    return pl.multiple_of(((shift // TILE + block) & (count - 1)) * TILE, TILE)


def order_of(base, shape, axis, shift, half):
    return (base + iota(shape, axis) - shift) & (half - 1)


def query_terms(place, bound, half):
    later = place >= bound
    length = jnp.where(later, half - bound, bound).astype(F32)
    return jnp.where(later, bound, 0), 1.0 / length


def attend_kernel(facts, x_ref, received_ref, y_hbm, att_hbm, stats_ref, y_ref, att_ref, y_sem, att_sems):
    core, shift, bound = facts[0], facts[1], facts[2]
    half = y_ref.shape[0]
    heads, rows, lanes = received_ref.shape
    quarter = heads // 2
    for s in range(quarter):
        for ref, side in ((x_ref, core), (received_ref, 1 - core)):
            upper = upper_rows(facts, side, s, (rows, lanes))
            at = pl.multiple_of((2 * s + side) * rows, rows)
            y_ref[pl.ds(at, rows), :] = choose(upper, ref[s], ref[s + quarter])

    stores = [pltpu.make_async_copy(y_ref, y_hbm, y_sem)]
    stores[0].start()
    hdim = 128
    scaling = hdim ** (-0.5)
    count = half // TILE
    for qi in range(count):
        base = block_base(qi, shift, count)
        span = pl.ds(base, TILE)
        place = order_of(base, (TILE, 1), 0, shift, half)
        first, inv_length = query_terms(place, bound, half)
        query = y_ref[span, 256:384]
        attention = 0.0
        for ki in needed_keys(qi, count):
            key_base = block_base(ki, shift, count)
            keys = pl.ds(key_base, TILE)
            scores = nt_dot(query, y_ref[keys, 384:512]) * scaling
            at = order_of(key_base, (1, TILE), 1, shift, half)
            allowed = (at <= place) & (at >= first)
            weights = jnp.where(
                allowed, scores * jax.nn.sigmoid(scores) * inv_length, 0.0
            ).astype(BF16)
            attention += nn_dot(weights, y_ref[keys, 128:256])

        att_ref[span, :] = attention
        stores.append(
            pltpu.make_async_copy(att_ref.at[span], att_hbm.at[span], att_sems.at[qi])
        )
        stores[-1].start()
        gated = y_ref[span, 0:128].astype(F32)
        center = jnp.mean(attention, axis=1, keepdims=True)
        shifted = attention - center
        columns = [
            center,
            jnp.sum(shifted * shifted, axis=1, keepdims=True),
            jnp.sum(gated, axis=1, keepdims=True),
            jnp.sum(gated * shifted, axis=1, keepdims=True),
        ]
        lane = iota((TILE, 128), 1)
        table = jnp.zeros((TILE, 128), F32)
        for i, column in enumerate(columns):
            table = jnp.where(lane == i, column, table)
        turned = table.T[0:4]
        for h in range(heads):
            stats_ref[h, :, span] = turned
    for store in stores:
        store.wait()


def backward_kernel(
    facts, y_hbm, att_hbm, stats_ref, mine_ref, send_ref, y_ref, att_ref, attn, grad, dq, dk, dv, sems
):
    core, shift, bound = facts[0], facts[1], facts[2]
    rows_in = [
        pltpu.make_async_copy(att_hbm, att_ref, sems.at[0]),
        pltpu.make_async_copy(y_hbm, y_ref, sems.at[1]),
    ]
    for load in rows_in:
        load.start()
    half = y_ref.shape[0]
    heads = stats_ref.shape[0]
    quarter, rows = mine_ref.shape[0], mine_ref.shape[1]
    hdim = 128
    width = heads * hdim
    count = half // TILE
    stat = [[stats_ref[h, i : i + 1, :] for i in range(4)] for h in range(heads)]
    mean = sum(s[0] for s in stat) / heads
    variance, mean_grad, mean_prod = 0.0, 0.0, 0.0
    for center, spread, grad_sum, prod_sum in stat:
        offset = center - mean
        variance += spread + hdim * offset * offset
        mean_grad += grad_sum
        mean_prod += prod_sum + offset * grad_sum
    inv_attn = lax.rsqrt(variance / width + EPSILON)
    line = iota((128, half), 0)
    table = jnp.where(
        line == 0,
        mean,
        jnp.where(
            line == 1,
            inv_attn,
            jnp.where(line == 2, mean_grad / width, inv_attn * mean_prod / width),
        ),
    )
    columns = table.T
    for load in rows_in:
        load.wait()
    for qi in range(count):
        span = slice(qi * TILE, (qi + 1) * TILE)
        inv = columns[span, 1:2]
        attn_norm = (att_ref[span, :] - columns[span, 0:1]) * inv
        gated = y_ref[span, 0:128].astype(F32)
        attn[span, :] = attn_norm.astype(BF16)
        grad[span, :] = (
            inv * (gated - columns[span, 2:3] - attn_norm * columns[span, 3:4])
        ).astype(BF16)
    dq[...] = jnp.zeros_like(dq)
    scaling = hdim ** (-0.5)
    for ki in range(count):
        key_base = block_base(ki, shift, count)
        keys = pl.ds(key_base, TILE)
        at = order_of(key_base, (TILE, 1), 0, shift, half)
        key, value = y_ref[keys, 384:512], y_ref[keys, 128:256]
        grad_key, grad_value = 0.0, 0.0
        for qi in range(count):
            if ki not in needed_keys(qi, count):
                continue
            base = block_base(qi, shift, count)
            span = pl.ds(base, TILE)
            place = order_of(base, (1, TILE), 1, shift, half)
            first, inv_length = query_terms(place, bound, half)
            query, grad_out = y_ref[span, 256:384], grad[span, :]
            scores = nt_dot(key, query) * scaling
            allowed = (at <= place) & (at >= first)
            sig = jax.nn.sigmoid(scores)
            product = scores * sig
            weights = jnp.where(allowed, product * inv_length, 0.0).astype(BF16)
            slope = (sig + product * (1.0 - sig)) * (inv_length * scaling)
            grad_weights = nt_dot(value, grad_out)
            grad_scores = jnp.where(allowed, grad_weights * slope, 0.0).astype(BF16)
            grad_value += nn_dot(weights, grad_out)
            grad_key += nn_dot(grad_scores, query)
            dq[span, :] += tn_dot(grad_scores, key)
        dk[keys, :] = grad_key.astype(BF16)
        dv[keys, :] = grad_value.astype(BF16)

    for s in range(quarter):
        near = pl.ds(pl.multiple_of((2 * s + core) * rows, rows), rows)
        far = pl.ds(pl.multiple_of((2 * s + 1 - core) * rows, rows), rows)
        for i, ref in enumerate((attn, dv, dq, dk)):
            columns = slice(i * hdim, (i + 1) * hdim)
            mine_ref[s, :, columns] = ref[near, :].astype(BF16)
            send_ref[s, :, columns] = ref[far, :].astype(BF16)


def finish_kernel(
    back_ref, proj_ref, mixed_ref, gate_ref, slot_ref, embed_ref, cot_ref, weight_hbm, out_ref, gated_ref, weight_ref, sems
):
    heads = back_ref.shape[0]
    width = embed_ref.shape[1]
    loads = copies(weight_hbm, weight_ref, sems, column_spans(4 * width, width))
    total = 0.0
    for t in range(4):
        loads[t].wait()
        for pair in range(heads // 2):
            columns = slice(pair * 256, (pair + 1) * 256)
            lanes = slice(t * 128, (t + 1) * 128)
            base = t * width + pair * 256
            grad_act = jnp.concatenate(
                [back_ref[2 * pair, :, lanes], back_ref[2 * pair + 1, :, lanes]], axis=1
            ).astype(F32)
            if t == 0:
                gated_ref[:, columns] = (grad_act * gate_ref[:, columns].astype(F32)).astype(BF16)
                grad_act = grad_act * mixed_ref[:, columns]
            projected = proj_ref[:, base : base + 256]
            sig = jax.nn.sigmoid(projected)
            slope = sig * (1.0 + projected * (1.0 - sig))
            total += nt_dot((grad_act * slope).astype(BF16), weight_ref[:, base : base + 256])
    normed, inv_embed = normalize(embed_ref[...])
    grad_embed = cot_ref[...].astype(F32) + normalize_back(total, normed, inv_embed)
    slots, rows = out_ref.shape[0], slot_ref.shape[1]
    place = jnp.where(slot_ref[...] == iota((slots, rows), 0), 1.0, 0.0).astype(BF16)
    out_ref[...] = nn_dot(place, grad_embed.astype(BF16)).astype(BF16)


def table_kernel(incoming_ref, arrived_ref, scale_ref, out_ref, buffer, sems):
    slots = arrived_ref.shape[0]
    steps = sems.shape[0]
    block = buffer.shape[0] // steps
    copies = []
    for n in range(steps):
        span = pl.ds(n * block, block)
        chosen = incoming_ref[...] - 1 - n * block == iota((block, slots), 0)
        total = nn_dot(jnp.where(chosen, 1.0, 0.0).astype(BF16), arrived_ref[...])
        scale = jnp.broadcast_to(scale_ref[:, span], (128, block)).T
        buffer[span, :] = total * scale[:, 0:1]
        copies.append(pltpu.make_async_copy(buffer.at[span], out_ref.at[span], sems.at[n]))
        copies[-1].start()
    for copy in copies:
        copy.wait()


def per_device(
    table_rows,
    row_scales,
    owners,
    shard_rows,
    history_lengths,
    input_weight,
    output_weight,
    cotangent,
):
    rows = owners.shape[0]
    table_size, width = table_rows.shape
    heads = HEADS
    hdim = width // heads
    devices = lax.axis_size(("dp", "cp"))
    n_cp = lax.axis_size("cp")
    cores = n_cp // heads
    half = rows * n_cp // 2
    quarter = heads // 2
    slots = devices * CAPACITY
    groups = [[i * cores + c for i in range(heads)] for c in range(cores)]
    swap = [(i, i ^ 1) for i in range(n_cp)]
    core = (lax.axis_index("cp") % cores).reshape(1)
    everyone = ("dp", "cp")
    shape = jax.ShapeDtypeStruct
    smem = pl.BlockSpec(memory_space=pltpu.SMEM)
    vmem = pl.BlockSpec(memory_space=pltpu.VMEM)
    hbm = pl.BlockSpec(memory_space=pltpu.HBM)

    def kernel(body, name, ins, outs, out_shape, mib, scratch=()):
        return pl.pallas_call(
            body,
            in_specs=ins,
            out_specs=outs,
            out_shape=out_shape,
            scratch_shapes=list(scratch),
            compiler_params=pltpu.CompilerParams(vmem_limit_bytes=mib << 20 if mib else None),
            name=name,
        )

    def exchange(values, axes, **options):
        return lax.all_to_all(values, axes, split_axis=0, concat_axis=0, tiled=True, **options)

    def to_heads(values):
        return exchange(values, "cp", axis_index_groups=groups)

    def to_all(values):
        lanes = values.shape[1]
        return exchange(values.reshape(devices, CAPACITY, lanes), everyone).reshape(slots, lanes)

    dma = pltpu.SemaphoreType.DMA

    def far(values):
        return pltpu.with_memory_space_constraint(values, pltpu.HBM)

    weight_far = far(input_weight)
    scale_line = row_scales.reshape(1, table_size)
    requests, slot_line, facts = kernel(
        request_kernel,
        "request",
        [smem, smem, vmem, vmem],
        (vmem, vmem, smem),
        (shape((devices, 128), I32), shape((1, rows), I32), shape((4,), I32)),
        0,
    )(core, history_lengths, owners.reshape(1, rows), shard_rows.reshape(1, rows))
    incoming = exchange(requests.reshape(devices, 1, 128), everyone).reshape(devices, 128)

    wide = width + 128
    fetched = kernel(
        fetch_kernel,
        "fetch",
        [vmem, hbm, vmem],
        vmem,
        shape((slots, wide), BF16),
        16,
        (pltpu.VMEM((table_size, width), BF16), dma((width // 512,))),
    )(incoming, far(table_rows), scale_line)
    returned = to_all(fetched)

    grad_mixed = jnp.einsum("rk,dk->rd", cotangent, output_weight, preferred_element_type=F32)

    near_weight = (pltpu.VMEM((width, 4 * width), BF16), dma((4,)))
    packed, projected, embedded, gate = kernel(
        project_kernel,
        "project",
        [vmem] * 3 + [hbm],
        (vmem, vmem, vmem, vmem),
        (
            shape((heads, rows, 4 * hdim), BF16),
            shape((rows, 4 * width), F32),
            shape((rows, width), F32),
            shape((rows, width), BF16),
        ),
        24,
        near_weight,
    )(returned, slot_line, grad_mixed, weight_far)

    branches = to_heads(packed)
    received = lax.ppermute(branches, "cp", swap)
    ordered, attention, stats = kernel(
        attend_kernel,
        "attend",
        [smem, vmem, vmem],
        (hbm, hbm, vmem),
        (
            pltpu.HBM((half, 4 * hdim), BF16),
            pltpu.HBM((half, hdim), F32),
            shape((heads, 4, half), F32),
        ),
        16,
        (
            pltpu.VMEM((half, 4 * hdim), BF16),
            pltpu.VMEM((half, hdim), F32),
            dma(()),
            dma((half // TILE,)),
        ),
    )(facts, branches, received)
    stats = to_heads(stats)

    backed = shape((quarter, rows, 4 * hdim), BF16)
    near = pltpu.VMEM((half, hdim), BF16)
    mine, send = kernel(
        backward_kernel,
        "backward",
        [smem, hbm, hbm, vmem],
        (vmem, vmem),
        (backed, backed),
        24,
        (pltpu.VMEM((half, 4 * hdim), BF16), pltpu.VMEM((half, hdim), F32))
        + (near, near, pltpu.VMEM((half, hdim), F32), near, near, dma((2,))),
    )(facts, far(ordered), far(attention), stats)
    received = lax.ppermute(send, "cp", swap)
    joined = kernel(
        join_kernel,
        "join",
        [smem, vmem, vmem],
        vmem,
        shape((heads, rows, 4 * hdim), BF16),
        8,
    )(facts, mine, received)
    back = to_heads(joined)

    outgoing, mixed = kernel(
        finish_kernel,
        "finish",
        [vmem] * 7 + [hbm],
        (vmem, vmem),
        (shape((slots, width), BF16), shape((rows, width), BF16)),
        24,
        near_weight,
    )(back, projected, grad_mixed, gate, slot_line, embedded, cotangent, weight_far)
    arrived = to_all(outgoing)
    layer_out = (
        embedded + jnp.dot(mixed, output_weight, preferred_element_type=F32)
    ).astype(BF16)

    table_grad = kernel(
        table_kernel,
        "table",
        [vmem] * 3,
        hbm,
        shape((table_size, width), F32),
        24,
        (pltpu.VMEM((table_size, width), F32), pltpu.SemaphoreType.DMA((16,))),
    )(incoming[:, :CAPACITY].reshape(1, slots), arrived, scale_line)
    return (layer_out, table_grad)


def solution(mesh):
    return jax.shard_map(
        per_device,
        mesh=mesh,
        in_specs=(
            P(("dp", "cp"), None),
            P(("dp", "cp")),
            P(("dp", "cp"), None),
            P(("dp", "cp")),
            P("dp", None),
            P(),
            P(),
            P(("dp", "cp"), None),
        ),
        out_specs=(P(("dp", "cp"), None), P(("dp", "cp"), None)),
        check_vma=False,
    )
```

```python
import jax
import jax.numpy as jnp
from jax import lax
from jax.experimental import pallas as pl
from jax.experimental.pallas import tpu as pltpu
from jax.sharding import PartitionSpec as P

HEADS = 8
EPSILON = 1e-05
CAPACITY = 2
TILE = 256
F32, BF16, I32 = jnp.float32, jnp.bfloat16, jnp.int32


def nt_dot(left, right):
    return lax.dot_general(left, right, (((1,), (1,)), ((), ())), preferred_element_type=F32)


def tn_dot(left, right):
    return lax.dot_general(left, right, (((0,), (0,)), ((), ())), preferred_element_type=F32)


def nn_dot(left, right):
    return jnp.dot(left, right, preferred_element_type=F32)


def copies(source, target, sems, spans):
    started = [
        pltpu.make_async_copy(source.at[span], target.at[span], sems.at[n])
        for n, span in enumerate(spans)
    ]
    for copy in started:
        copy.start()
    return started


def column_spans(total, step):
    return [(slice(None), slice(base, base + step)) for base in range(0, total, step)]


def iota(shape, axis):
    return lax.broadcasted_iota(I32, shape, axis)


def silu_parts(half_value):
    twice = 1.0 + jnp.tanh(half_value)
    return twice, half_value * twice


def normalize(values):
    center = jnp.mean(values, axis=-1, keepdims=True)
    shifted = values - center
    inv_spread = lax.rsqrt(jnp.mean(shifted * shifted, axis=-1, keepdims=True) + EPSILON)
    return (shifted * inv_spread, inv_spread)


def normalize_back(grad_in, normed, inv_spread):
    return inv_spread * (
        grad_in
        - jnp.mean(grad_in, axis=-1, keepdims=True)
        - normed * jnp.mean(grad_in * normed, axis=-1, keepdims=True)
    )


def request_kernel(core_ref, lengths_ref, owner_ref, row_ref, request_ref, slot_ref, facts_ref):
    shape = request_ref.shape
    match = owner_ref[...] == iota(shape, 0)
    earlier = jnp.where(iota(shape, 0) < iota(shape, 1), 1.0, 0.0).astype(BF16)
    before = nn_dot(jnp.where(match, 1.0, 0.0).astype(BF16), earlier)
    rank = jnp.sum(jnp.where(match, before, 0.0), axis=0, keepdims=True).astype(I32)
    slot_ref[...] = owner_ref[...] * CAPACITY + rank
    wanted = row_ref[...].astype(F32) + 1.0
    lists = [
        jnp.sum(jnp.where(match & (before == c), wanted, 0.0), axis=1, keepdims=True)
        for c in range(CAPACITY)
    ]
    lane = iota(shape, 1)
    request_ref[...] = jnp.where(
        lane == 0, lists[0], jnp.where(lane == 1, lists[1], 0.0)
    ).astype(I32)
    core = core_ref[0]
    one, two, three = lengths_ref[0, 0], lengths_ref[0, 1], lengths_ref[0, 2]
    half = (one + two + three) // 2
    most = jnp.maximum(one, jnp.maximum(two, three))
    longest = jnp.where(one == most, 0, jnp.where(two == most, one, one + two))
    inner = jnp.where(one == most, two, one)
    facts_ref[0] = core
    facts_ref[1] = jnp.where(core == 0, longest & (half - 1), 0)
    facts_ref[2] = jnp.where(core == 0, 0, inner)
    facts_ref[3] = longest


def split_scale(scale):
    high = scale.astype(BF16).astype(F32)
    rest = scale - high
    middle = rest.astype(BF16).astype(F32)
    return high, middle, rest - middle


def fetch_kernel(incoming_ref, table_hbm, scale_hbm, out_ref, table_ref, scale_ref, sems, scale_sem):
    scale_load = pltpu.make_async_copy(scale_hbm, scale_ref, scale_sem)
    scale_load.start()
    loads = copies(table_hbm, table_ref, sems, column_spans(table_ref.shape[1], 512))
    slots, size, width = out_ref.shape[0], table_ref.shape[0], table_ref.shape[1]
    devices = slots // CAPACITY
    device_of = iota((slots, devices), 0) >> 1 == iota((slots, devices), 1)
    spread = jnp.where(device_of, 1.0, 0.0).astype(BF16)
    wanted = incoming_ref[...]
    high = nn_dot(spread, (wanted >> 4).astype(F32).astype(BF16))
    low = nn_dot(spread, (wanted & 15).astype(F32).astype(BF16))
    mine = iota((slots, 128), 1) == (iota((slots, 128), 0) & 1)
    row = jnp.sum(jnp.where(mine, high * 16.0 + low, 0.0), axis=1, keepdims=True)
    chosen = row.astype(I32) - 1 == iota((slots, size), 1)
    hot = jnp.where(chosen, 1.0, 0.0).astype(BF16)
    scale_load.wait()
    scale = jnp.sum(jnp.where(chosen, scale_ref[...], 0.0), axis=1, keepdims=True)
    high, middle, low = split_scale(scale)
    lane = iota((slots, 128), 1)
    pieces = jnp.where(
        lane == 0, high, jnp.where(lane == 1, middle, jnp.where(lane == 2, low, 0.0))
    )
    out_ref[:, width : width + 128] = pieces.astype(BF16)
    for n, base in enumerate(range(0, width, 512)):
        loads[n].wait()
        out_ref[:, base : base + 512] = nn_dot(hot, table_ref[:, base : base + 512]).astype(BF16)


def mix_kernel(cot_ref, weight_ref, out_ref):
    out_ref[...] = nt_dot(cot_ref[...], weight_ref[...])


def output_kernel(embed_ref, mixed_ref, weight_ref, out_ref):
    out_ref[...] = (embed_ref[...] + nn_dot(mixed_ref[...], weight_ref[...])).astype(BF16)


def project_kernel(
    returned_ref, slot_ref, mixed_ref, weight_hbm, packed_ref, proj_ref, embed_ref, gate_ref, weight_ref, sems
):
    width = embed_ref.shape[1]
    loads = copies(weight_hbm, weight_ref, sems, column_spans(4 * width, width))
    heads = packed_ref.shape[0]
    slots, rows = returned_ref.shape[0], slot_ref.shape[1]
    place = jnp.where(slot_ref[...] == iota((slots, rows), 0), 1.0, 0.0).astype(BF16)
    total = tn_dot(place, returned_ref[...])
    scale = total[:, width : width + 1] + (
        total[:, width + 1 : width + 2] + total[:, width + 2 : width + 3]
    )
    embedded = total[:, :width] * scale
    embed_ref[...] = embedded
    normed = normalize(embedded)[0].astype(BF16)
    for t in range(4):
        loads[t].wait()
        for pair in range(heads // 2):
            columns = slice(pair * 256, (pair + 1) * 256)
            base = t * width + pair * 256
            projected = nn_dot(normed, weight_ref[:, base : base + 256])
            proj_ref[:, base : base + 256] = projected
            active = silu_parts(0.5 * projected)[1].astype(BF16)
            if t == 0:
                gate_ref[:, columns] = active
                active = (active.astype(F32) * mixed_ref[:, columns]).astype(BF16)
            for i in range(2):
                packed_ref[2 * pair + i, :, t * 128 : (t + 1) * 128] = active[
                    :, i * 128 : (i + 1) * 128
                ]


def upper_rows(facts, core, s, shape):
    rows = shape[0]
    residue = s * 2 * rows + core * rows + iota(shape, 0)
    return (jnp.where(residue >= facts[3], 1, 0) ^ facts[0]) == 1


def choose(mask, yes, no):
    return jnp.where(mask, yes.astype(F32), no.astype(F32)).astype(BF16)


def join_kernel(facts, mine_ref, received_ref, out_ref):
    quarter = mine_ref.shape[0]
    for s in range(quarter):
        upper = upper_rows(facts, facts[0], s, mine_ref.shape[1:])
        out_ref[s] = choose(upper, mine_ref[s], received_ref[s])
        out_ref[s + quarter] = choose(upper, received_ref[s], mine_ref[s])


def rows_of(facts, s, side, rows, half):
    start = ((s - facts[1] // TILE) & (half // TILE - 1)) * TILE + side * rows
    return pl.ds(pl.multiple_of(start, rows), rows)


def share_of(facts, query_base, keys, half):
    seam, bound = facts[1] & (TILE - 1), facts[2]
    place = (query_base + iota((1, TILE), 1) - seam) & (half - 1)
    later = place >= bound
    first = jnp.where(later, bound, 0)
    inv_length = 1.0 / jnp.where(later, half - bound, bound).astype(F32)
    at = (iota((keys, 1), 0) - seam) & (half - 1)
    return jnp.where((at <= place) & (at >= first), inv_length, 0.0)


def blocks_of(half):
    for base in range(0, half, TILE):
        yield base, (half if base == 0 else base + TILE)


def attend_kernel(
    facts, x_ref, received_ref, y_ref, att_ref, grad_ref, stats_ref, turned
):
    core = facts[0]
    half, lanes = y_ref.shape
    heads, rows = received_ref.shape[0], received_ref.shape[1]
    quarter = heads // 2
    hdim = att_ref.shape[0]
    for s in range(quarter):
        for ref, side in ((x_ref, core), (received_ref, 1 - core)):
            upper = upper_rows(facts, side, s, (rows, lanes))
            y_ref[rows_of(facts, s, side, rows, half), :] = choose(upper, ref[s], ref[s + quarter])
    for base in range(0, half, TILE):
        span = slice(base, base + TILE)
        grad_ref[:, span] = y_ref[span, 0:128].astype(F32).T.astype(BF16)
        turned[:, span] = y_ref[span, 128:256].astype(F32).T.astype(BF16)
    for base, keys in blocks_of(half):
        span = slice(base, base + TILE)
        half_scores = nt_dot(y_ref[0:keys, 384:512], y_ref[span, 256:384]) * (0.5 * hdim**-0.5)
        weights = (silu_parts(half_scores)[1] * share_of(facts, base, keys, half)).astype(BF16)
        attention = nn_dot(turned[:, 0:keys], weights)
        att_ref[:, span] = attention
        gated = grad_ref[:, span].astype(F32)
        center = jnp.mean(attention, axis=0, keepdims=True)
        shifted = attention - center
        lines = [
            center,
            jnp.sum(shifted * shifted, axis=0, keepdims=True),
            jnp.sum(gated, axis=0, keepdims=True),
            jnp.sum(gated * shifted, axis=0, keepdims=True),
        ]
        line = iota((8, TILE), 0)
        table = jnp.zeros((8, TILE), F32)
        for i, values in enumerate(lines):
            table = jnp.where(line == i, values, table)
        for h in range(heads):
            stats_ref[h, :, span] = table[0:4]


def backward_kernel(
    facts, y_ref, att_ref, gated_ref, stats_ref, mine_ref, send_ref, attn, grad, dq, dk, dv
):
    core = facts[0]
    half = y_ref.shape[0]
    heads = stats_ref.shape[0]
    quarter, rows = mine_ref.shape[0], mine_ref.shape[1]
    hdim = att_ref.shape[0]
    width = heads * hdim
    stat = [[stats_ref[h, i : i + 1, :] for i in range(4)] for h in range(heads)]
    mean = sum(s[0] for s in stat) / heads
    variance, mean_grad, mean_prod = 0.0, 0.0, 0.0
    for center, spread, grad_sum, prod_sum in stat:
        offset = center - mean
        variance += spread + hdim * offset * offset
        mean_grad += grad_sum
        mean_prod += prod_sum + offset * grad_sum
    inv_attn = lax.rsqrt(variance / width + EPSILON)
    mean_grad = mean_grad / width
    mean_prod = inv_attn * mean_prod / width
    for base in range(0, half, TILE):
        span = slice(base, base + TILE)
        inv = inv_attn[:, span]
        attn_norm = (att_ref[:, span] - mean[:, span]) * inv
        attn[span, :] = attn_norm.T.astype(BF16)
        gated = gated_ref[:, span].astype(F32)
        grad[:, span] = (
            inv * (gated - mean_grad[:, span] - attn_norm * mean_prod[:, span])
        ).astype(BF16)
    scaling = 0.5 * hdim**-0.5
    for base, keys in blocks_of(half):
        span = slice(base, base + TILE)
        key, query, grad_out = y_ref[0:keys, 384:512], y_ref[span, 256:384], grad[:, span]
        share = share_of(facts, base, keys, half)
        twice, product = silu_parts(nt_dot(key, query) * scaling)
        weights = (product * share).astype(BF16)
        slope = (twice + product * (2.0 - twice)) * share
        grad_scores = (nn_dot(y_ref[0:keys, 128:256], grad_out) * slope).astype(BF16)
        grad_value = nt_dot(weights, grad_out)
        grad_key = nn_dot(grad_scores, query)
        dq[span, :] = (tn_dot(grad_scores, key) * scaling).astype(BF16)
        if base == 0:
            dv[...] = grad_value
            dk[...] = grad_key
        else:
            dv[0:keys, :] += grad_value
            dk[0:keys, :] += grad_key
    for s in range(quarter):
        for out_ref, side in ((mine_ref, core), (send_ref, 1 - core)):
            at = rows_of(facts, s, side, rows, half)
            parts = (attn[at, :], dv[at, :], dq[at, :], dk[at, :] * scaling)
            for i, part in enumerate(parts):
                out_ref[s, :, i * hdim : (i + 1) * hdim] = part.astype(BF16)


def finish_kernel(
    back_ref, proj_ref, mixed_ref, gate_ref, slot_ref, embed_ref, cot_ref, weight_hbm, out_ref, gated_hbm, weight_ref, gated_ref, sems, sem
):
    heads = back_ref.shape[0]
    width = embed_ref.shape[1]
    loads = copies(weight_hbm, weight_ref, sems, column_spans(4 * width, width))
    total = 0.0
    for t in range(4):
        loads[t].wait()
        for pair in range(heads // 2):
            columns = slice(pair * 256, (pair + 1) * 256)
            lanes = slice(t * 128, (t + 1) * 128)
            base = t * width + pair * 256
            grad_act = jnp.concatenate(
                [back_ref[2 * pair, :, lanes], back_ref[2 * pair + 1, :, lanes]], axis=1
            ).astype(F32)
            if t == 0:
                gated_ref[:, columns] = (grad_act * gate_ref[:, columns].astype(F32)).astype(BF16)
                grad_act = grad_act * mixed_ref[:, columns]
            projected = proj_ref[:, base : base + 256]
            twice, active = silu_parts(0.5 * projected)
            slope = 0.5 * (twice + active * (2.0 - twice))
            total += nt_dot((grad_act * slope).astype(BF16), weight_ref[:, base : base + 256])
    store = pltpu.make_async_copy(gated_ref, gated_hbm, sem)
    store.start()
    normed, inv_embed = normalize(embed_ref[...])
    grad_embed = cot_ref[...].astype(F32) + normalize_back(total, normed, inv_embed)
    slots, rows = out_ref.shape[0], slot_ref.shape[1]
    place = jnp.where(slot_ref[...] == iota((slots, rows), 0), 1.0, 0.0).astype(BF16)
    out_ref[...] = nn_dot(place, grad_embed.astype(BF16)).astype(BF16)
    store.wait()


def table_kernel(incoming_ref, arrived_ref, scale_ref, out_ref, buffer, sems):
    slots = arrived_ref.shape[0]
    steps = sems.shape[0]
    block = buffer.shape[0] // steps
    copies = []
    for n in range(steps):
        span = pl.ds(n * block, block)
        chosen = incoming_ref[...] - 1 - n * block == iota((block, slots), 0)
        total = nn_dot(jnp.where(chosen, 1.0, 0.0).astype(BF16), arrived_ref[...])
        scale = jnp.broadcast_to(scale_ref[:, span], (128, block)).T
        buffer[span, :] = total * scale[:, 0:1]
        copies.append(pltpu.make_async_copy(buffer.at[span], out_ref.at[span], sems.at[n]))
        copies[-1].start()
    for copy in copies:
        copy.wait()


def per_device(
    table_rows,
    row_scales,
    owners,
    shard_rows,
    history_lengths,
    input_weight,
    output_weight,
    cotangent,
):
    rows = owners.shape[0]
    table_size, width = table_rows.shape
    heads = HEADS
    hdim = width // heads
    devices = lax.axis_size(("dp", "cp"))
    n_cp = lax.axis_size("cp")
    cores = n_cp // heads
    half = rows * n_cp // 2
    quarter = heads // 2
    slots = devices * CAPACITY
    groups = [[i * cores + c for i in range(heads)] for c in range(cores)]
    swap = [(i, i ^ 1) for i in range(n_cp)]
    core = (lax.axis_index("cp") % cores).reshape(1)
    everyone = ("dp", "cp")
    shape = jax.ShapeDtypeStruct
    smem = pl.BlockSpec(memory_space=pltpu.SMEM)
    vmem = pl.BlockSpec(memory_space=pltpu.VMEM)
    hbm = pl.BlockSpec(memory_space=pltpu.HBM)

    def kernel(body, name, ins, outs, out_shape, mib, scratch=()):
        return pl.pallas_call(
            body,
            in_specs=ins,
            out_specs=outs,
            out_shape=out_shape,
            scratch_shapes=list(scratch),
            compiler_params=pltpu.CompilerParams(vmem_limit_bytes=mib << 20 if mib else None),
            name=name,
        )

    def exchange(values, axes, **options):
        return lax.all_to_all(values, axes, split_axis=0, concat_axis=0, tiled=True, **options)

    def to_heads(values):
        return exchange(values, "cp", axis_index_groups=groups)

    def to_all(values):
        lanes = values.shape[1]
        return exchange(values.reshape(devices, CAPACITY, lanes), everyone).reshape(slots, lanes)

    dma = pltpu.SemaphoreType.DMA

    def far(values):
        return pltpu.with_memory_space_constraint(values, pltpu.HBM)

    weight_far = far(input_weight)
    scale_line = row_scales.reshape(1, table_size)
    requests, slot_line, facts = kernel(
        request_kernel,
        "request",
        [smem, smem, vmem, vmem],
        (vmem, vmem, smem),
        (shape((devices, 128), I32), shape((1, rows), I32), shape((4,), I32)),
        0,
    )(core, history_lengths, owners.reshape(1, rows), shard_rows.reshape(1, rows))
    incoming = exchange(requests.reshape(devices, 1, 128), everyone).reshape(devices, 128)

    wide = width + 128
    fetched = kernel(
        fetch_kernel,
        "fetch",
        [vmem, hbm, hbm],
        vmem,
        shape((slots, wide), BF16),
        16,
        (
            pltpu.VMEM((table_size, width), BF16),
            pltpu.VMEM((1, table_size), F32),
            dma((width // 512,)),
            dma(()),
        ),
    )(incoming, far(table_rows), far(scale_line))
    returned = to_all(fetched)

    output_far = far(output_weight)
    grad_mixed = kernel(
        mix_kernel, "mix", [vmem] * 2, vmem, shape((rows, width), F32), 8
    )(cotangent, output_far)

    near_weight = (pltpu.VMEM((width, 4 * width), BF16), dma((4,)))
    packed, projected, embedded, gate = kernel(
        project_kernel,
        "project",
        [vmem] * 3 + [hbm],
        (vmem, vmem, vmem, vmem),
        (
            shape((heads, rows, 4 * hdim), BF16),
            shape((rows, 4 * width), F32),
            shape((rows, width), F32),
            shape((rows, width), BF16),
        ),
        24,
        near_weight,
    )(returned, slot_line, grad_mixed, weight_far)

    branches = to_heads(packed)
    received = lax.ppermute(branches, "cp", swap)
    ordered, attention, gated, stats = kernel(
        attend_kernel,
        "attend",
        [smem, vmem, vmem],
        (vmem, vmem, vmem, vmem),
        (
            shape((half, 4 * hdim), BF16),
            shape((hdim, half), F32),
            shape((hdim, half), BF16),
            shape((heads, 4, half), F32),
        ),
        16,
        (pltpu.VMEM((hdim, half), BF16),),
    )(facts, branches, received)
    stats = to_heads(stats)

    backed = shape((quarter, rows, 4 * hdim), BF16)
    mine, send = kernel(
        backward_kernel,
        "backward",
        [smem, vmem, vmem, vmem, vmem],
        (vmem, vmem),
        (backed, backed),
        24,
        (
            pltpu.VMEM((half, hdim), BF16),
            pltpu.VMEM((hdim, half), BF16),
            pltpu.VMEM((half, hdim), BF16),
            pltpu.VMEM((half, hdim), F32),
            pltpu.VMEM((half, hdim), F32),
        ),
    )(facts, ordered, attention, gated, stats)
    received = lax.ppermute(send, "cp", swap)
    joined = kernel(
        join_kernel,
        "join",
        [smem, vmem, vmem],
        vmem,
        shape((heads, rows, 4 * hdim), BF16),
        8,
    )(facts, mine, received)
    back = to_heads(joined)

    outgoing, mixed = kernel(
        finish_kernel,
        "finish",
        [vmem] * 7 + [hbm],
        (vmem, hbm),
        (shape((slots, width), BF16), pltpu.HBM((rows, width), BF16)),
        24,
        (near_weight[0], pltpu.VMEM((rows, width), BF16), near_weight[1], dma(())),
    )(back, projected, grad_mixed, gate, slot_line, embedded, cotangent, weight_far)
    arrived = to_all(outgoing)
    layer_out = kernel(
        output_kernel, "output", [vmem] * 3, vmem, shape((rows, width), BF16), 8
    )(embedded, mixed, output_far)

    table_grad = kernel(
        table_kernel,
        "table",
        [vmem] * 3,
        hbm,
        shape((table_size, width), F32),
        24,
        (pltpu.VMEM((table_size, width), F32), pltpu.SemaphoreType.DMA((16,))),
    )(incoming[:, :CAPACITY].reshape(1, slots), arrived, scale_line)
    return (layer_out, table_grad)


def solution(mesh):
    return jax.shard_map(
        per_device,
        mesh=mesh,
        in_specs=(
            P(("dp", "cp"), None),
            P(("dp", "cp")),
            P(("dp", "cp"), None),
            P(("dp", "cp")),
            P("dp", None),
            P(),
            P(),
            P(("dp", "cp"), None),
        ),
        out_specs=(P(("dp", "cp"), None), P(("dp", "cp"), None)),
        check_vma=False,
    )
```

```python
import jax
import jax.numpy as jnp
from jax import lax
from jax.experimental import pallas as pl
from jax.experimental.pallas import tpu as pltpu
from jax.sharding import PartitionSpec as P

HEADS = 8
EPSILON = 1e-05
CAPACITY = 2
TILE = 256
F32, BF16, I32 = jnp.float32, jnp.bfloat16, jnp.int32


def nt_dot(left, right):
    return lax.dot_general(left, right, (((1,), (1,)), ((), ())), preferred_element_type=F32)


def tn_dot(left, right):
    return lax.dot_general(left, right, (((0,), (0,)), ((), ())), preferred_element_type=F32)


def nn_dot(left, right):
    return jnp.dot(left, right, preferred_element_type=F32)


def parts_of(source, target, sems, first, axis):
    loads = []
    step = target.shape[axis] // sems.shape[0]
    for n in range(sems.shape[0]):
        begin, span = [slice(None)] * 2, [slice(None)] * 2
        begin[axis], span[axis] = pl.ds(first + n * step, step), pl.ds(n * step, step)
        loads.append(
            pltpu.make_async_copy(source.at[tuple(begin)], target.at[tuple(span)], sems.at[n])
        )
        loads[n].start()
    return loads


def iota(shape, axis):
    return lax.broadcasted_iota(I32, shape, axis)


def silu_parts(half_value):
    twice = 1.0 + jnp.tanh(half_value)
    return twice, half_value * twice


def normalize(values):
    center = jnp.mean(values, axis=-1, keepdims=True)
    shifted = values - center
    inv_spread = lax.rsqrt(jnp.mean(shifted * shifted, axis=-1, keepdims=True) + EPSILON)
    return (shifted * inv_spread, inv_spread)


def normalize_back(grad_in, normed, inv_spread):
    return inv_spread * (
        grad_in
        - jnp.mean(grad_in, axis=-1, keepdims=True)
        - normed * jnp.mean(grad_in * normed, axis=-1, keepdims=True)
    )


def request_kernel(core_ref, lengths_ref, owner_ref, row_ref, request_ref, slot_ref, facts_ref):
    shape = request_ref.shape
    match = owner_ref[...] == iota(shape, 0)
    earlier = jnp.where(iota(shape, 0) < iota(shape, 1), 1.0, 0.0).astype(BF16)
    before = nn_dot(jnp.where(match, 1.0, 0.0).astype(BF16), earlier)
    rank = jnp.sum(jnp.where(match, before, 0.0), axis=0, keepdims=True).astype(I32)
    slot_ref[...] = owner_ref[...] * CAPACITY + rank
    wanted = row_ref[...].astype(F32) + 1.0
    lists = [
        jnp.sum(jnp.where(match & (before == c), wanted, 0.0), axis=1, keepdims=True)
        for c in range(CAPACITY)
    ]
    lane = iota(shape, 1)
    request_ref[...] = jnp.where(
        lane == 0, lists[0], jnp.where(lane == 1, lists[1], 0.0)
    ).astype(I32)
    core = core_ref[0]
    one, two, three = lengths_ref[0, 0], lengths_ref[0, 1], lengths_ref[0, 2]
    half = (one + two + three) // 2
    most = jnp.maximum(one, jnp.maximum(two, three))
    longest = jnp.where(one == most, 0, jnp.where(two == most, one, one + two))
    inner = jnp.where(one == most, two, one)
    facts_ref[0] = core
    facts_ref[1] = jnp.where(core == 0, longest & (half - 1), 0)
    facts_ref[2] = jnp.where(core == 0, 0, inner)
    facts_ref[3] = longest


def split_scale(scale):
    high = scale.astype(BF16).astype(F32)
    rest = scale - high
    middle = rest.astype(BF16).astype(F32)
    return high, middle, rest - middle


def fetch_kernel(incoming_ref, upper_ref, table_hbm, scale_hbm, out_ref, lower_ref, scale_ref, sems, scale_sem):
    scale_load = pltpu.make_async_copy(scale_hbm, scale_ref, scale_sem)
    scale_load.start()
    upper, width = upper_ref.shape
    loads = parts_of(table_hbm, lower_ref, sems, upper, 0)
    size = scale_ref.shape[1]
    slots = out_ref.shape[0] * CAPACITY
    devices = slots // CAPACITY
    device_of = iota((slots, devices), 0) >> 1 == iota((slots, devices), 1)
    spread = jnp.where(device_of, 1.0, 0.0).astype(BF16)
    wanted = incoming_ref[...]
    high = nn_dot(spread, (wanted >> 4).astype(F32).astype(BF16))
    low = nn_dot(spread, (wanted & 15).astype(F32).astype(BF16))
    mine = iota((slots, 128), 1) == (iota((slots, 128), 0) & 1)
    row = jnp.sum(jnp.where(mine, high * 16.0 + low, 0.0), axis=1, keepdims=True)
    chosen = row.astype(I32) - 1 == iota((slots, size), 1)
    hot = jnp.where(chosen, 1.0, 0.0).astype(BF16)
    scale_load.wait()
    scale = jnp.sum(jnp.where(chosen, scale_ref[...], 0.0), axis=1, keepdims=True)
    high, middle, low = split_scale(scale)
    lane = iota((slots, 128), 1)
    pieces = jnp.where(
        lane == 0, high, jnp.where(lane == 1, middle, jnp.where(lane == 2, low, 0.0))
    )
    out_ref[:, :, width : width + 128] = pieces.astype(BF16).reshape(devices, CAPACITY, 128)
    for load in loads:
        load.wait()
    for base in range(0, width, 256):
        columns = slice(base, base + 256)
        rows = nn_dot(hot[:, :upper], upper_ref[:, columns])
        rows += nn_dot(hot[:, upper:], lower_ref[:, columns])
        out_ref[:, :, columns] = rows.astype(BF16).reshape(devices, CAPACITY, 256)


def mix_kernel(cot_ref, weight_ref, out_ref):
    out_ref[...] = nt_dot(cot_ref[...], weight_ref[...])


def output_kernel(embed_ref, mixed_ref, weight_ref, out_ref):
    out_ref[...] = (embed_ref[...] + nn_dot(mixed_ref[...], weight_ref[...])).astype(BF16)


def project_kernel(
    returned_ref, slot_ref, mixed_ref, weight_hbm, packed_ref, proj_ref, embed_ref, gate_ref, weight_ref, sems
):
    width = embed_ref.shape[1]
    loads = parts_of(weight_hbm, weight_ref, sems, 0, 1)
    heads = packed_ref.shape[0]
    devices, capacity, wide = returned_ref.shape
    slots, rows = devices * capacity, slot_ref.shape[1]
    place = jnp.where(slot_ref[...] == iota((slots, rows), 0), 1.0, 0.0).astype(BF16)
    total = tn_dot(place, returned_ref[...].reshape(slots, wide))
    scale = total[:, width : width + 1] + (
        total[:, width + 1 : width + 2] + total[:, width + 2 : width + 3]
    )
    embedded = total[:, :width] * scale
    embed_ref[...] = embedded
    normed = normalize(embedded)[0].astype(BF16)
    for t in range(4):
        loads[t].wait()
        for pair in range(heads // 2):
            columns = slice(pair * 256, (pair + 1) * 256)
            base = t * width + pair * 256
            projected = nn_dot(normed, weight_ref[:, base : base + 256])
            proj_ref[:, base : base + 256] = projected
            active = silu_parts(0.5 * projected)[1].astype(BF16)
            if t == 0:
                gate_ref[:, columns] = active
                active = (active.astype(F32) * mixed_ref[:, columns]).astype(BF16)
            for i in range(2):
                packed_ref[2 * pair + i, :, t * 128 : (t + 1) * 128] = active[
                    :, i * 128 : (i + 1) * 128
                ]


def upper_rows(facts, core, s, shape):
    rows = shape[0]
    residue = s * 2 * rows + core * rows + iota(shape, 0)
    return (jnp.where(residue >= facts[3], 1, 0) ^ facts[0]) == 1


def choose(mask, yes, no):
    return jnp.where(mask, yes.astype(F32), no.astype(F32)).astype(BF16)


def join_kernel(facts, mine_ref, received_ref, out_ref):
    quarter = mine_ref.shape[0]
    for s in range(quarter):
        upper = upper_rows(facts, facts[0], s, mine_ref.shape[1:])
        out_ref[s] = choose(upper, mine_ref[s], received_ref[s])
        out_ref[s + quarter] = choose(upper, received_ref[s], mine_ref[s])


def rows_of(facts, s, side, rows, half):
    start = ((s - facts[1] // TILE) & (half // TILE - 1)) * TILE + side * rows
    return pl.ds(pl.multiple_of(start, rows), rows)


def share_of(facts, query_base, keys, half):
    seam, bound = facts[1] & (TILE - 1), facts[2]
    place = (query_base + iota((1, TILE), 1) - seam) & (half - 1)
    later = place >= bound
    first = jnp.where(later, bound, 0)
    inv_length = 1.0 / jnp.where(later, half - bound, bound).astype(F32)
    at = (iota((keys, 1), 0) - seam) & (half - 1)
    return jnp.where((at <= place) & (at >= first), inv_length, 0.0)


def blocks_of(half):
    for base in range(0, half, TILE):
        yield base, (half if base == 0 else base + TILE)


def attend_kernel(
    facts, x_ref, received_ref, y_ref, att_ref, grad_ref, stats_ref, turned
):
    core = facts[0]
    half, lanes = y_ref.shape
    heads, rows = received_ref.shape[0], received_ref.shape[1]
    quarter = heads // 2
    hdim = att_ref.shape[0]
    for s in range(quarter):
        for ref, side in ((x_ref, core), (received_ref, 1 - core)):
            upper = upper_rows(facts, side, s, (rows, lanes))
            y_ref[rows_of(facts, s, side, rows, half), :] = choose(upper, ref[s], ref[s + quarter])
    for base in range(0, half, TILE):
        span = slice(base, base + TILE)
        grad_ref[:, span] = y_ref[span, 0:128].astype(F32).T.astype(BF16)
        turned[:, span] = y_ref[span, 128:256].astype(F32).T.astype(BF16)
    for base, keys in blocks_of(half):
        span = slice(base, base + TILE)
        half_scores = nt_dot(y_ref[0:keys, 384:512], y_ref[span, 256:384]) * (0.5 * hdim**-0.5)
        weights = (silu_parts(half_scores)[1] * share_of(facts, base, keys, half)).astype(BF16)
        attention = nn_dot(turned[:, 0:keys], weights)
        att_ref[:, span] = attention
        gated = grad_ref[:, span].astype(F32)
        center = jnp.mean(attention, axis=0, keepdims=True)
        shifted = attention - center
        lines = [
            center,
            jnp.sum(shifted * shifted, axis=0, keepdims=True),
            jnp.sum(gated, axis=0, keepdims=True),
            jnp.sum(gated * shifted, axis=0, keepdims=True),
        ]
        line = iota((8, TILE), 0)
        table = jnp.zeros((8, TILE), F32)
        for i, values in enumerate(lines):
            table = jnp.where(line == i, values, table)
        for h in range(heads):
            stats_ref[h, :, span] = table[0:4]


def backward_kernel(
    facts, y_ref, att_ref, gated_ref, stats_ref, mine_ref, send_ref, attn, grad, dq, dk, dv
):
    core = facts[0]
    half = y_ref.shape[0]
    heads = stats_ref.shape[0]
    quarter, rows = mine_ref.shape[0], mine_ref.shape[1]
    hdim = att_ref.shape[0]
    width = heads * hdim
    stat = [[stats_ref[h, i : i + 1, :] for i in range(4)] for h in range(heads)]
    mean = sum(s[0] for s in stat) / heads
    variance, mean_grad, mean_prod = 0.0, 0.0, 0.0
    for center, spread, grad_sum, prod_sum in stat:
        offset = center - mean
        variance += spread + hdim * offset * offset
        mean_grad += grad_sum
        mean_prod += prod_sum + offset * grad_sum
    inv_attn = lax.rsqrt(variance / width + EPSILON)
    mean_grad = mean_grad / width
    mean_prod = inv_attn * mean_prod / width
    for base in range(0, half, TILE):
        span = slice(base, base + TILE)
        inv = inv_attn[:, span]
        attn_norm = (att_ref[:, span] - mean[:, span]) * inv
        attn[span, :] = attn_norm.T.astype(BF16)
        gated = gated_ref[:, span].astype(F32)
        grad[:, span] = (
            inv * (gated - mean_grad[:, span] - attn_norm * mean_prod[:, span])
        ).astype(BF16)
    scaling = 0.5 * hdim**-0.5
    for base, keys in blocks_of(half):
        span = slice(base, base + TILE)
        key, query, grad_out = y_ref[0:keys, 384:512], y_ref[span, 256:384], grad[:, span]
        share = share_of(facts, base, keys, half)
        twice, product = silu_parts(nt_dot(key, query) * scaling)
        weights = (product * share).astype(BF16)
        slope = (twice + product * (2.0 - twice)) * share
        grad_scores = (nn_dot(y_ref[0:keys, 128:256], grad_out) * slope).astype(BF16)
        grad_value = nt_dot(weights, grad_out)
        grad_key = nn_dot(grad_scores, query)
        dq[span, :] = (tn_dot(grad_scores, key) * scaling).astype(BF16)
        if base == 0:
            dv[...] = grad_value
            dk[...] = grad_key
        else:
            dv[0:keys, :] += grad_value
            dk[0:keys, :] += grad_key
    for s in range(quarter):
        for out_ref, side in ((mine_ref, core), (send_ref, 1 - core)):
            at = rows_of(facts, s, side, rows, half)
            parts = (attn[at, :], dv[at, :], dq[at, :], dk[at, :] * scaling)
            for i, part in enumerate(parts):
                out_ref[s, :, i * hdim : (i + 1) * hdim] = part.astype(BF16)


def finish_kernel(
    back_ref, proj_ref, mixed_ref, gate_ref, slot_ref, embed_ref, cot_ref, weight_hbm, out_ref, gated_hbm, weight_ref, gated_ref, sems, sem
):
    heads = back_ref.shape[0]
    width = embed_ref.shape[1]
    loads = parts_of(weight_hbm, weight_ref, sems, 0, 1)
    total = 0.0
    for t in range(4):
        loads[t].wait()
        for pair in range(heads // 2):
            columns = slice(pair * 256, (pair + 1) * 256)
            lanes = slice(t * 128, (t + 1) * 128)
            base = t * width + pair * 256
            grad_act = jnp.concatenate(
                [back_ref[2 * pair, :, lanes], back_ref[2 * pair + 1, :, lanes]], axis=1
            ).astype(F32)
            if t == 0:
                gated_ref[:, columns] = (grad_act * gate_ref[:, columns].astype(F32)).astype(BF16)
                grad_act = grad_act * mixed_ref[:, columns]
            projected = proj_ref[:, base : base + 256]
            twice, active = silu_parts(0.5 * projected)
            slope = 0.5 * (twice + active * (2.0 - twice))
            total += nt_dot((grad_act * slope).astype(BF16), weight_ref[:, base : base + 256])
    store = pltpu.make_async_copy(gated_ref, gated_hbm, sem)
    store.start()
    normed, inv_embed = normalize(embed_ref[...])
    grad_embed = cot_ref[...].astype(F32) + normalize_back(total, normed, inv_embed)
    slots, rows = out_ref.shape[0] * out_ref.shape[1], slot_ref.shape[1]
    place = jnp.where(slot_ref[...] == iota((slots, rows), 0), 1.0, 0.0).astype(BF16)
    out_ref[...] = nn_dot(place, grad_embed.astype(BF16)).astype(BF16).reshape(out_ref.shape)
    store.wait()


def table_kernel(incoming_ref, arrived_ref, scale_ref, out_ref, buffer, sems):
    devices, capacity, width = arrived_ref.shape
    slots = devices * capacity
    arrived = arrived_ref[...].reshape(slots, width)
    steps = sems.shape[0]
    block = buffer.shape[0] // steps
    copies = []
    for n in range(steps):
        span = pl.ds(n * block, block)
        chosen = incoming_ref[...] - 1 - n * block == iota((block, slots), 0)
        total = nn_dot(jnp.where(chosen, 1.0, 0.0).astype(BF16), arrived)
        scale = jnp.broadcast_to(scale_ref[:, span], (128, block)).T
        buffer[span, :] = total * scale[:, 0:1]
        copies.append(pltpu.make_async_copy(buffer.at[span], out_ref.at[span], sems.at[n]))
        copies[-1].start()
    for copy in copies:
        copy.wait()


def per_device(
    table_rows,
    row_scales,
    owners,
    shard_rows,
    history_lengths,
    input_weight,
    output_weight,
    cotangent,
):
    rows = owners.shape[0]
    table_size, width = table_rows.shape
    heads = HEADS
    hdim = width // heads
    devices = lax.axis_size(("dp", "cp"))
    n_cp = lax.axis_size("cp")
    cores = n_cp // heads
    half = rows * n_cp // 2
    quarter = heads // 2
    slots = devices * CAPACITY
    groups = [[i * cores + c for i in range(heads)] for c in range(cores)]
    swap = [(i, i ^ 1) for i in range(n_cp)]
    core = (lax.axis_index("cp") % cores).reshape(1)
    everyone = ("dp", "cp")
    shape = jax.ShapeDtypeStruct
    smem = pl.BlockSpec(memory_space=pltpu.SMEM)
    vmem = pl.BlockSpec(memory_space=pltpu.VMEM)
    hbm = pl.BlockSpec(memory_space=pltpu.HBM)

    def kernel(body, name, ins, outs, out_shape, mib, scratch=()):
        return pl.pallas_call(
            body,
            in_specs=ins,
            out_specs=outs,
            out_shape=out_shape,
            scratch_shapes=list(scratch),
            compiler_params=pltpu.CompilerParams(vmem_limit_bytes=mib << 20 if mib else None),
            name=name,
        )

    def exchange(values, axes, **options):
        return lax.all_to_all(values, axes, split_axis=0, concat_axis=0, tiled=True, **options)

    def to_heads(values):
        return exchange(values, "cp", axis_index_groups=groups)

    def to_all(values):
        return exchange(values, everyone)

    dma = pltpu.SemaphoreType.DMA

    def far(values):
        return pltpu.with_memory_space_constraint(values, pltpu.HBM)

    def near(values):
        return pltpu.with_memory_space_constraint(values, pltpu.VMEM)

    weight_far = far(input_weight)
    scale_line = row_scales.reshape(1, table_size)
    requests, slot_line, facts = kernel(
        request_kernel,
        "request",
        [smem, smem, vmem, vmem],
        (vmem, vmem, smem),
        (shape((devices, 128), I32), shape((1, rows), I32), shape((4,), I32)),
        0,
    )(core, history_lengths, owners.reshape(1, rows), shard_rows.reshape(1, rows))
    incoming = exchange(requests.reshape(devices, 1, 128), everyone).reshape(devices, 128)

    wide = width + 128
    fetched = kernel(
        fetch_kernel,
        "fetch",
        [vmem, vmem, hbm, hbm],
        vmem,
        shape((devices, CAPACITY, wide), BF16),
        16,
        (
            pltpu.VMEM((table_size // 2, width), BF16),
            pltpu.VMEM((1, table_size), F32),
            dma((2,)),
            dma(()),
        ),
    )(incoming, near(table_rows[: table_size // 2]), far(table_rows), far(scale_line))
    returned = to_all(fetched)

    output_far = far(output_weight)
    grad_mixed = kernel(
        mix_kernel, "mix", [vmem] * 2, vmem, shape((rows, width), F32), 8
    )(cotangent, output_far)

    near_weight = (pltpu.VMEM((width, 4 * width), BF16), dma((4,)))
    packed, projected, embedded, gate = kernel(
        project_kernel,
        "project",
        [vmem] * 3 + [hbm],
        (vmem, vmem, vmem, vmem),
        (
            shape((heads, rows, 4 * hdim), BF16),
            shape((rows, 4 * width), F32),
            shape((rows, width), F32),
            shape((rows, width), BF16),
        ),
        24,
        near_weight,
    )(returned, slot_line, grad_mixed, weight_far)

    branches = to_heads(packed)
    received = lax.ppermute(branches, "cp", swap)
    ordered, attention, gated, stats = kernel(
        attend_kernel,
        "attend",
        [smem, vmem, vmem],
        (vmem, vmem, vmem, vmem),
        (
            shape((half, 4 * hdim), BF16),
            shape((hdim, half), F32),
            shape((hdim, half), BF16),
            shape((heads, 4, half), F32),
        ),
        16,
        (pltpu.VMEM((hdim, half), BF16),),
    )(facts, branches, received)
    stats = to_heads(stats)

    backed = shape((quarter, rows, 4 * hdim), BF16)
    mine, send = kernel(
        backward_kernel,
        "backward",
        [smem, vmem, vmem, vmem, vmem],
        (vmem, vmem),
        (backed, backed),
        24,
        (
            pltpu.VMEM((half, hdim), BF16),
            pltpu.VMEM((hdim, half), BF16),
            pltpu.VMEM((half, hdim), BF16),
            pltpu.VMEM((half, hdim), F32),
            pltpu.VMEM((half, hdim), F32),
        ),
    )(facts, ordered, attention, gated, stats)
    received = lax.ppermute(send, "cp", swap)
    joined = kernel(
        join_kernel,
        "join",
        [smem, vmem, vmem],
        vmem,
        shape((heads, rows, 4 * hdim), BF16),
        8,
    )(facts, mine, received)
    back = to_heads(joined)

    outgoing, mixed = kernel(
        finish_kernel,
        "finish",
        [vmem] * 7 + [hbm],
        (vmem, hbm),
        (shape((devices, CAPACITY, width), BF16), pltpu.HBM((rows, width), BF16)),
        24,
        (near_weight[0], pltpu.VMEM((rows, width), BF16), near_weight[1], dma(())),
    )(back, projected, grad_mixed, gate, slot_line, embedded, cotangent, weight_far)
    arrived = to_all(outgoing)
    layer_out = kernel(
        output_kernel, "output", [vmem] * 3, vmem, shape((rows, width), BF16), 8
    )(embedded, mixed, output_far)

    table_grad = kernel(
        table_kernel,
        "table",
        [vmem] * 3,
        hbm,
        shape((table_size, width), F32),
        24,
        (pltpu.VMEM((table_size, width), F32), pltpu.SemaphoreType.DMA((16,))),
    )(incoming[:, :CAPACITY].reshape(1, slots), arrived, scale_line)
    return (layer_out, table_grad)


def solution(mesh):
    return jax.shard_map(
        per_device,
        mesh=mesh,
        in_specs=(
            P(("dp", "cp"), None),
            P(("dp", "cp")),
            P(("dp", "cp"), None),
            P(("dp", "cp")),
            P("dp", None),
            P(),
            P(),
            P(("dp", "cp"), None),
        ),
        out_specs=(P(("dp", "cp"), None), P(("dp", "cp"), None)),
        check_vma=False,
    )
```

```python
import jax
import jax.numpy as jnp
from jax import lax
from jax.experimental import pallas as pl
from jax.experimental.pallas import tpu as pltpu
from jax.sharding import PartitionSpec as P

HEADS = 8
EPSILON = 1e-05
CAPACITY = 2
TILE = 256
F32, BF16, I32 = jnp.float32, jnp.bfloat16, jnp.int32


def nt_dot(left, right):
    return lax.dot_general(left, right, (((1,), (1,)), ((), ())), preferred_element_type=F32)


def tn_dot(left, right):
    return lax.dot_general(left, right, (((0,), (0,)), ((), ())), preferred_element_type=F32)


def nn_dot(left, right):
    return jnp.dot(left, right, preferred_element_type=F32)


def parts_of(source, target, sems, first, axis):
    loads = []
    step = target.shape[axis] // sems.shape[0]
    for n in range(sems.shape[0]):
        begin, span = [slice(None)] * 2, [slice(None)] * 2
        begin[axis], span[axis] = pl.ds(first + n * step, step), pl.ds(n * step, step)
        loads.append(
            pltpu.make_async_copy(source.at[tuple(begin)], target.at[tuple(span)], sems.at[n])
        )
        loads[n].start()
    return loads


def iota(shape, axis):
    return lax.broadcasted_iota(I32, shape, axis)


def silu_parts(half_value):
    twice = 1.0 + jnp.tanh(half_value)
    return twice, half_value * twice


def normalize(values):
    center = jnp.mean(values, axis=-1, keepdims=True)
    shifted = values - center
    inv_spread = lax.rsqrt(jnp.mean(shifted * shifted, axis=-1, keepdims=True) + EPSILON)
    return (shifted * inv_spread, inv_spread)


def normalize_back(grad_in, normed, inv_spread):
    return inv_spread * (
        grad_in
        - jnp.mean(grad_in, axis=-1, keepdims=True)
        - normed * jnp.mean(grad_in * normed, axis=-1, keepdims=True)
    )


def request_kernel(core_ref, lengths_ref, owner_ref, row_ref, request_ref, slot_ref, facts_ref):
    shape = request_ref.shape
    match = owner_ref[...] == iota(shape, 0)
    earlier = jnp.where(iota(shape, 0) < iota(shape, 1), 1.0, 0.0).astype(BF16)
    before = nn_dot(jnp.where(match, 1.0, 0.0).astype(BF16), earlier)
    rank = jnp.sum(jnp.where(match, before, 0.0), axis=0, keepdims=True).astype(I32)
    slot_ref[...] = owner_ref[...] * CAPACITY + rank
    wanted = row_ref[...].astype(F32) + 1.0
    lists = [
        jnp.sum(jnp.where(match & (before == c), wanted, 0.0), axis=1, keepdims=True)
        for c in range(CAPACITY)
    ]
    lane = iota(shape, 1)
    request_ref[...] = jnp.where(
        lane == 0, lists[0], jnp.where(lane == 1, lists[1], 0.0)
    ).astype(I32)
    core = core_ref[0]
    one, two, three = lengths_ref[0, 0], lengths_ref[0, 1], lengths_ref[0, 2]
    half = (one + two + three) // 2
    most = jnp.maximum(one, jnp.maximum(two, three))
    longest = jnp.where(one == most, 0, jnp.where(two == most, one, one + two))
    inner = jnp.where(one == most, two, one)
    facts_ref[0] = core
    facts_ref[1] = jnp.where(core == 0, longest & (half - 1), 0)
    facts_ref[2] = jnp.where(core == 0, 0, inner)
    facts_ref[3] = longest


def split_scale(scale):
    high = scale.astype(BF16).astype(F32)
    rest = scale - high
    middle = rest.astype(BF16).astype(F32)
    return high, middle, rest - middle


def fetch_kernel(
    incoming_ref, upper_ref, table_hbm, scale_hbm, out_hbm, lower_ref, scale_ref, out_ref, sems, scale_sem, out_sems
):
    scale_load = pltpu.make_async_copy(scale_hbm, scale_ref, scale_sem)
    scale_load.start()
    upper, width = upper_ref.shape
    loads = parts_of(table_hbm, lower_ref, sems, upper, 0)
    size = scale_ref.shape[1]
    slots = out_ref.shape[0] * CAPACITY
    devices = slots // CAPACITY
    device_of = iota((slots, devices), 0) >> 1 == iota((slots, devices), 1)
    spread = jnp.where(device_of, 1.0, 0.0).astype(BF16)
    wanted = incoming_ref[...]
    high = nn_dot(spread, (wanted >> 4).astype(F32).astype(BF16))
    low = nn_dot(spread, (wanted & 15).astype(F32).astype(BF16))
    mine = iota((slots, 128), 1) == (iota((slots, 128), 0) & 1)
    row = jnp.sum(jnp.where(mine, high * 16.0 + low, 0.0), axis=1, keepdims=True)
    chosen = row.astype(I32) - 1 == iota((slots, size), 1)
    hot = jnp.where(chosen, 1.0, 0.0).astype(BF16)
    scale_load.wait()
    scale = jnp.sum(jnp.where(chosen, scale_ref[...], 0.0), axis=1, keepdims=True)
    high, middle, low = split_scale(scale)
    lane = iota((slots, 128), 1)
    pieces = jnp.where(
        lane == 0, high, jnp.where(lane == 1, middle, jnp.where(lane == 2, low, 0.0))
    )
    out_ref[:, :, width : width + 128] = pieces.astype(BF16).reshape(devices, CAPACITY, 128)
    for load in loads:
        load.wait()
    stores = []
    for base in range(0, width, 256):
        columns = slice(base, base + 256)
        rows = nn_dot(hot[:, :upper], upper_ref[:, columns])
        rows += nn_dot(hot[:, upper:], lower_ref[:, columns])
        out_ref[:, :, columns] = rows.astype(BF16).reshape(devices, CAPACITY, 256)
        columns = slice(base, base + 256 if base + 256 < width else width + 128)
        stores.append(
            pltpu.make_async_copy(
                out_ref.at[:, :, columns], out_hbm.at[:, :, columns], out_sems.at[base // 256]
            )
        )
        stores[-1].start()
    for store in stores:
        store.wait()


def mix_kernel(cot_ref, weight_ref, out_ref):
    out_ref[...] = nt_dot(cot_ref[...], weight_ref[...])


def output_kernel(embed_ref, mixed_ref, weight_ref, out_ref):
    out_ref[...] = (embed_ref[...] + nn_dot(mixed_ref[...], weight_ref[...])).astype(BF16)


def project_kernel(
    returned_ref, slot_ref, mixed_ref, weight_hbm, packed_ref, proj_ref, embed_ref, gate_ref, weight_ref, sems
):
    width = embed_ref.shape[1]
    loads = parts_of(weight_hbm, weight_ref, sems, 0, 1)
    heads = packed_ref.shape[0]
    devices, capacity, wide = returned_ref.shape
    slots, rows = devices * capacity, slot_ref.shape[1]
    place = jnp.where(slot_ref[...] == iota((slots, rows), 0), 1.0, 0.0).astype(BF16)
    total = tn_dot(place, returned_ref[...].reshape(slots, wide))
    scale = total[:, width : width + 1] + (
        total[:, width + 1 : width + 2] + total[:, width + 2 : width + 3]
    )
    embedded = total[:, :width] * scale
    embed_ref[...] = embedded
    normed = normalize(embedded)[0].astype(BF16)
    for t in range(4):
        loads[t].wait()
        for pair in range(heads // 2):
            columns = slice(pair * 256, (pair + 1) * 256)
            base = t * width + pair * 256
            projected = nn_dot(normed, weight_ref[:, base : base + 256])
            proj_ref[:, base : base + 256] = projected
            active = silu_parts(0.5 * projected)[1].astype(BF16)
            if t == 0:
                gate_ref[:, columns] = active
                active = (active.astype(F32) * mixed_ref[:, columns]).astype(BF16)
            for i in range(2):
                packed_ref[2 * pair + i, :, t * 128 : (t + 1) * 128] = active[
                    :, i * 128 : (i + 1) * 128
                ]


def upper_rows(facts, core, s, shape):
    rows = shape[0]
    residue = s * 2 * rows + core * rows + iota(shape, 0)
    return (jnp.where(residue >= facts[3], 1, 0) ^ facts[0]) == 1


def choose(mask, yes, no):
    return jnp.where(mask, yes.astype(F32), no.astype(F32)).astype(BF16)


def join_kernel(facts, mine_ref, received_ref, out_ref):
    quarter = mine_ref.shape[0]
    for s in range(quarter):
        upper = upper_rows(facts, facts[0], s, mine_ref.shape[1:])
        out_ref[s] = choose(upper, mine_ref[s], received_ref[s])
        out_ref[s + quarter] = choose(upper, received_ref[s], mine_ref[s])


def rows_of(facts, s, side, rows, half):
    start = ((s - facts[1] // TILE) & (half // TILE - 1)) * TILE + side * rows
    return pl.ds(pl.multiple_of(start, rows), rows)


def share_of(facts, query_base, keys, half):
    seam, bound = facts[1] & (TILE - 1), facts[2]
    place = (query_base + iota((1, TILE), 1) - seam) & (half - 1)
    later = place >= bound
    first = jnp.where(later, bound, 0)
    inv_length = 1.0 / jnp.where(later, half - bound, bound).astype(F32)
    at = (iota((keys, 1), 0) - seam) & (half - 1)
    return jnp.where((at <= place) & (at >= first), inv_length, 0.0)


def blocks_of(half):
    for base in range(0, half, TILE):
        yield base, (half if base == 0 else base + TILE)


def attend_kernel(
    facts, x_ref, received_ref, y_ref, att_ref, grad_ref, stats_ref, turned
):
    core = facts[0]
    half, lanes = y_ref.shape
    heads, rows = received_ref.shape[0], received_ref.shape[1]
    quarter = heads // 2
    hdim = att_ref.shape[0]
    for s in range(quarter):
        for ref, side in ((x_ref, core), (received_ref, 1 - core)):
            upper = upper_rows(facts, side, s, (rows, lanes))
            y_ref[rows_of(facts, s, side, rows, half), :] = choose(upper, ref[s], ref[s + quarter])
    for base in range(0, half, TILE):
        span = slice(base, base + TILE)
        grad_ref[:, span] = y_ref[span, 0:128].astype(F32).T.astype(BF16)
        turned[:, span] = y_ref[span, 128:256].astype(F32).T.astype(BF16)
    for base, keys in blocks_of(half):
        span = slice(base, base + TILE)
        half_scores = nt_dot(y_ref[0:keys, 384:512], y_ref[span, 256:384]) * (0.5 * hdim**-0.5)
        weights = (silu_parts(half_scores)[1] * share_of(facts, base, keys, half)).astype(BF16)
        attention = nn_dot(turned[:, 0:keys], weights)
        att_ref[:, span] = attention
        gated = grad_ref[:, span].astype(F32)
        center = jnp.mean(attention, axis=0, keepdims=True)
        shifted = attention - center
        lines = [
            center,
            jnp.sum(shifted * shifted, axis=0, keepdims=True),
            jnp.sum(gated, axis=0, keepdims=True),
            jnp.sum(gated * shifted, axis=0, keepdims=True),
        ]
        line = iota((8, TILE), 0)
        table = jnp.zeros((8, TILE), F32)
        for i, values in enumerate(lines):
            table = jnp.where(line == i, values, table)
        for h in range(heads):
            stats_ref[h, :, span] = table[0:4]


def backward_kernel(
    facts, y_ref, att_ref, gated_ref, stats_ref, mine_ref, send_ref, attn, grad, dq, dk, dv
):
    core = facts[0]
    half = y_ref.shape[0]
    heads = stats_ref.shape[0]
    quarter, rows = mine_ref.shape[0], mine_ref.shape[1]
    hdim = att_ref.shape[0]
    width = heads * hdim
    stat = [[stats_ref[h, i : i + 1, :] for i in range(4)] for h in range(heads)]
    mean = sum(s[0] for s in stat) / heads
    variance, mean_grad, mean_prod = 0.0, 0.0, 0.0
    for center, spread, grad_sum, prod_sum in stat:
        offset = center - mean
        variance += spread + hdim * offset * offset
        mean_grad += grad_sum
        mean_prod += prod_sum + offset * grad_sum
    inv_attn = lax.rsqrt(variance / width + EPSILON)
    mean_grad = mean_grad / width
    mean_prod = inv_attn * mean_prod / width
    for base in range(0, half, TILE):
        span = slice(base, base + TILE)
        inv = inv_attn[:, span]
        attn_norm = (att_ref[:, span] - mean[:, span]) * inv
        attn[span, :] = attn_norm.T.astype(BF16)
        gated = gated_ref[:, span].astype(F32)
        grad[:, span] = (
            inv * (gated - mean_grad[:, span] - attn_norm * mean_prod[:, span])
        ).astype(BF16)
    scaling = 0.5 * hdim**-0.5
    for base, keys in blocks_of(half):
        span = slice(base, base + TILE)
        key, query, grad_out = y_ref[0:keys, 384:512], y_ref[span, 256:384], grad[:, span]
        share = share_of(facts, base, keys, half)
        twice, product = silu_parts(nt_dot(key, query) * scaling)
        weights = (product * share).astype(BF16)
        slope = (twice + product * (2.0 - twice)) * share
        grad_scores = (nn_dot(y_ref[0:keys, 128:256], grad_out) * slope).astype(BF16)
        grad_value = nt_dot(weights, grad_out)
        grad_key = nn_dot(grad_scores, query)
        dq[span, :] = (tn_dot(grad_scores, key) * scaling).astype(BF16)
        if base == 0:
            dv[...] = grad_value
            dk[...] = grad_key
        else:
            dv[0:keys, :] += grad_value
            dk[0:keys, :] += grad_key
    for s in range(quarter):
        for out_ref, side in ((mine_ref, core), (send_ref, 1 - core)):
            at = rows_of(facts, s, side, rows, half)
            parts = (attn[at, :], dv[at, :], dq[at, :], dk[at, :] * scaling)
            for i, part in enumerate(parts):
                out_ref[s, :, i * hdim : (i + 1) * hdim] = part.astype(BF16)


def finish_kernel(
    back_ref, proj_ref, mixed_ref, gate_ref, slot_ref, embed_ref, cot_ref, weight_hbm, out_hbm, gated_hbm, weight_ref, gated_ref, out_ref, sems, sem, out_sems
):
    heads = back_ref.shape[0]
    width = embed_ref.shape[1]
    loads = parts_of(weight_hbm, weight_ref, sems, 0, 1)
    normed, inv_embed = normalize(embed_ref[...])
    cotangent = cot_ref[...].astype(F32)
    slots, rows = out_ref.shape[0] * out_ref.shape[1], slot_ref.shape[1]
    place = jnp.where(slot_ref[...] == iota((slots, rows), 0), 1.0, 0.0).astype(BF16)
    total = 0.0
    for t in range(4):
        loads[t].wait()
        for pair in range(heads // 2):
            columns = slice(pair * 256, (pair + 1) * 256)
            lanes = slice(t * 128, (t + 1) * 128)
            base = t * width + pair * 256
            grad_act = jnp.concatenate(
                [back_ref[2 * pair, :, lanes], back_ref[2 * pair + 1, :, lanes]], axis=1
            ).astype(F32)
            if t == 0:
                gated_ref[:, columns] = (grad_act * gate_ref[:, columns].astype(F32)).astype(BF16)
                grad_act = grad_act * mixed_ref[:, columns]
            projected = proj_ref[:, base : base + 256]
            twice, active = silu_parts(0.5 * projected)
            slope = 0.5 * (twice + active * (2.0 - twice))
            total += nt_dot((grad_act * slope).astype(BF16), weight_ref[:, base : base + 256])
    stores = [pltpu.make_async_copy(gated_ref, gated_hbm, sem)]
    stores[0].start()
    grad_embed = cotangent + normalize_back(total, normed, inv_embed)
    grad_embed = grad_embed.astype(BF16)
    for n in range(out_sems.shape[0]):
        step = width // out_sems.shape[0]
        columns = slice(n * step, (n + 1) * step)
        placed = nn_dot(place, grad_embed[:, columns]).astype(BF16)
        out_ref[:, :, columns] = placed.reshape(out_ref.shape[0], out_ref.shape[1], step)
        stores.append(
            pltpu.make_async_copy(
                out_ref.at[:, :, columns], out_hbm.at[:, :, columns], out_sems.at[n]
            )
        )
        stores[-1].start()
    for store in stores:
        store.wait()


def table_kernel(incoming_ref, arrived_ref, scale_ref, out_ref, buffer, sems):
    devices, capacity, width = arrived_ref.shape
    slots = devices * capacity
    arrived = arrived_ref[...].reshape(slots, width)
    steps = sems.shape[0]
    block = buffer.shape[0] // steps
    copies = []
    for n in range(steps):
        span = pl.ds(n * block, block)
        chosen = incoming_ref[...] - 1 - n * block == iota((block, slots), 0)
        total = nn_dot(jnp.where(chosen, 1.0, 0.0).astype(BF16), arrived)
        scale = jnp.broadcast_to(scale_ref[:, span], (128, block)).T
        buffer[span, :] = total * scale[:, 0:1]
        copies.append(pltpu.make_async_copy(buffer.at[span], out_ref.at[span], sems.at[n]))
        copies[-1].start()
    for copy in copies:
        copy.wait()


def per_device(
    table_rows,
    row_scales,
    owners,
    shard_rows,
    history_lengths,
    input_weight,
    output_weight,
    cotangent,
):
    rows = owners.shape[0]
    table_size, width = table_rows.shape
    heads = HEADS
    hdim = width // heads
    devices = lax.axis_size(("dp", "cp"))
    n_cp = lax.axis_size("cp")
    cores = n_cp // heads
    half = rows * n_cp // 2
    quarter = heads // 2
    slots = devices * CAPACITY
    groups = [[i * cores + c for i in range(heads)] for c in range(cores)]
    swap = [(i, i ^ 1) for i in range(n_cp)]
    core = (lax.axis_index("cp") % cores).reshape(1)
    everyone = ("dp", "cp")
    shape = jax.ShapeDtypeStruct
    smem = pl.BlockSpec(memory_space=pltpu.SMEM)
    vmem = pl.BlockSpec(memory_space=pltpu.VMEM)
    hbm = pl.BlockSpec(memory_space=pltpu.HBM)

    def kernel(body, name, ins, outs, out_shape, mib, scratch=()):
        return pl.pallas_call(
            body,
            in_specs=ins,
            out_specs=outs,
            out_shape=out_shape,
            scratch_shapes=list(scratch),
            compiler_params=pltpu.CompilerParams(vmem_limit_bytes=mib << 20 if mib else None),
            name=name,
        )

    def exchange(values, axes, **options):
        return lax.all_to_all(values, axes, split_axis=0, concat_axis=0, tiled=True, **options)

    def to_heads(values):
        return exchange(values, "cp", axis_index_groups=groups)

    def to_all(values):
        return exchange(values, everyone)

    dma = pltpu.SemaphoreType.DMA

    def far(values):
        return pltpu.with_memory_space_constraint(values, pltpu.HBM)

    def near(values):
        return pltpu.with_memory_space_constraint(values, pltpu.VMEM)

    weight_far = far(input_weight)
    scale_line = row_scales.reshape(1, table_size)
    requests, slot_line, facts = kernel(
        request_kernel,
        "request",
        [smem, smem, vmem, vmem],
        (vmem, vmem, smem),
        (shape((devices, 128), I32), shape((1, rows), I32), shape((4,), I32)),
        0,
    )(core, history_lengths, owners.reshape(1, rows), shard_rows.reshape(1, rows))
    incoming = exchange(requests.reshape(devices, 1, 128), everyone).reshape(devices, 128)

    wide = width + 128
    ahead = table_size * 5 // 8
    fetched = kernel(
        fetch_kernel,
        "fetch",
        [vmem, vmem, hbm, hbm],
        hbm,
        pltpu.HBM((devices, CAPACITY, wide), BF16),
        16,
        (
            pltpu.VMEM((table_size - ahead, width), BF16),
            pltpu.VMEM((1, table_size), F32),
            pltpu.VMEM((devices, CAPACITY, wide), BF16),
            dma((2,)),
            dma(()),
            dma((width // 256,)),
        ),
    )(incoming, near(table_rows[:ahead]), far(table_rows), far(scale_line))
    returned = to_all(fetched)

    output_far = far(output_weight)
    grad_mixed = kernel(
        mix_kernel, "mix", [vmem] * 2, vmem, shape((rows, width), F32), 8
    )(cotangent, output_far)

    near_weight = (pltpu.VMEM((width, 4 * width), BF16), dma((4,)))
    packed, projected, embedded, gate = kernel(
        project_kernel,
        "project",
        [vmem] * 3 + [hbm],
        (vmem, vmem, vmem, vmem),
        (
            shape((heads, rows, 4 * hdim), BF16),
            shape((rows, 4 * width), F32),
            shape((rows, width), F32),
            shape((rows, width), BF16),
        ),
        24,
        near_weight,
    )(returned, slot_line, grad_mixed, weight_far)

    branches = to_heads(packed)
    received = lax.ppermute(branches, "cp", swap)
    ordered, attention, gated, stats = kernel(
        attend_kernel,
        "attend",
        [smem, vmem, vmem],
        (vmem, vmem, vmem, vmem),
        (
            shape((half, 4 * hdim), BF16),
            shape((hdim, half), F32),
            shape((hdim, half), BF16),
            shape((heads, 4, half), F32),
        ),
        16,
        (pltpu.VMEM((hdim, half), BF16),),
    )(facts, branches, received)
    stats = to_heads(stats)

    backed = shape((quarter, rows, 4 * hdim), BF16)
    mine, send = kernel(
        backward_kernel,
        "backward",
        [smem, vmem, vmem, vmem, vmem],
        (vmem, vmem),
        (backed, backed),
        24,
        (
            pltpu.VMEM((half, hdim), BF16),
            pltpu.VMEM((hdim, half), BF16),
            pltpu.VMEM((half, hdim), BF16),
            pltpu.VMEM((half, hdim), F32),
            pltpu.VMEM((half, hdim), F32),
        ),
    )(facts, ordered, attention, gated, stats)
    received = lax.ppermute(send, "cp", swap)
    joined = kernel(
        join_kernel,
        "join",
        [smem, vmem, vmem],
        vmem,
        shape((heads, rows, 4 * hdim), BF16),
        8,
    )(facts, mine, received)
    back = to_heads(joined)

    outgoing, mixed = kernel(
        finish_kernel,
        "finish",
        [vmem] * 7 + [hbm],
        (hbm, hbm),
        (pltpu.HBM((devices, CAPACITY, width), BF16), pltpu.HBM((rows, width), BF16)),
        24,
        (
            near_weight[0],
            pltpu.VMEM((rows, width), BF16),
            pltpu.VMEM((devices, CAPACITY, width), BF16),
            near_weight[1],
            dma(()),
            dma((2,)),
        ),
    )(back, projected, grad_mixed, gate, slot_line, embedded, cotangent, weight_far)
    arrived = to_all(outgoing)
    layer_out = kernel(
        output_kernel, "output", [vmem] * 3, vmem, shape((rows, width), BF16), 8
    )(embedded, mixed, output_far)

    table_grad = kernel(
        table_kernel,
        "table",
        [vmem] * 3,
        hbm,
        shape((table_size, width), F32),
        24,
        (pltpu.VMEM((table_size, width), F32), pltpu.SemaphoreType.DMA((16,))),
    )(incoming[:, :CAPACITY].reshape(1, slots), arrived, scale_line)
    return (layer_out, table_grad)


def solution(mesh):
    return jax.shard_map(
        per_device,
        mesh=mesh,
        in_specs=(
            P(("dp", "cp"), None),
            P(("dp", "cp")),
            P(("dp", "cp"), None),
            P(("dp", "cp")),
            P("dp", None),
            P(),
            P(),
            P(("dp", "cp"), None),
        ),
        out_specs=(P(("dp", "cp"), None), P(("dp", "cp"), None)),
        check_vma=False,
    )
```

```python
import jax
import jax.numpy as jnp
from jax import lax
from jax.experimental import pallas as pl
from jax.experimental.pallas import tpu as pltpu
from jax.sharding import PartitionSpec as P

HEADS = 8
EPSILON = 1e-05
CAPACITY = 2
TILE = 256
F32, BF16, I32 = jnp.float32, jnp.bfloat16, jnp.int32


def nt_dot(left, right):
    return lax.dot_general(left, right, (((1,), (1,)), ((), ())), preferred_element_type=F32)


def tn_dot(left, right):
    return lax.dot_general(left, right, (((0,), (0,)), ((), ())), preferred_element_type=F32)


def nn_dot(left, right):
    return jnp.dot(left, right, preferred_element_type=F32)


def parts_of(source, target, sems, first, axis):
    loads = []
    step = target.shape[axis] // sems.shape[0]
    for n in range(sems.shape[0]):
        begin, span = [slice(None)] * 2, [slice(None)] * 2
        begin[axis], span[axis] = pl.ds(first + n * step, step), pl.ds(n * step, step)
        loads.append(
            pltpu.make_async_copy(source.at[tuple(begin)], target.at[tuple(span)], sems.at[n])
        )
        loads[n].start()
    return loads


def iota(shape, axis):
    return lax.broadcasted_iota(I32, shape, axis)


def silu_parts(half_value):
    twice = 1.0 + jnp.tanh(half_value)
    return twice, half_value * twice


def normalize(values):
    center = jnp.mean(values, axis=-1, keepdims=True)
    shifted = values - center
    inv_spread = lax.rsqrt(jnp.mean(shifted * shifted, axis=-1, keepdims=True) + EPSILON)
    return (shifted * inv_spread, inv_spread)


def normalize_back(grad_in, normed, inv_spread):
    return inv_spread * (
        grad_in
        - jnp.mean(grad_in, axis=-1, keepdims=True)
        - normed * jnp.mean(grad_in * normed, axis=-1, keepdims=True)
    )


def request_kernel(core_ref, lengths_ref, owner_ref, row_ref, request_ref, slot_ref, facts_ref):
    shape = request_ref.shape
    match = owner_ref[...] == iota(shape, 0)
    earlier = jnp.where(iota(shape, 0) < iota(shape, 1), 1.0, 0.0).astype(BF16)
    before = nn_dot(jnp.where(match, 1.0, 0.0).astype(BF16), earlier)
    rank = jnp.sum(jnp.where(match, before, 0.0), axis=0, keepdims=True).astype(I32)
    slot_ref[...] = owner_ref[...] * CAPACITY + rank
    wanted = row_ref[...].astype(F32) + 1.0
    lists = [
        jnp.sum(jnp.where(match & (before == c), wanted, 0.0), axis=1, keepdims=True)
        for c in range(CAPACITY)
    ]
    lane = iota(shape, 1)
    request_ref[...] = jnp.where(
        lane == 0, lists[0], jnp.where(lane == 1, lists[1], 0.0)
    ).astype(I32)
    core = core_ref[0]
    one, two, three = lengths_ref[0, 0], lengths_ref[0, 1], lengths_ref[0, 2]
    half = (one + two + three) // 2
    most = jnp.maximum(one, jnp.maximum(two, three))
    longest = jnp.where(one == most, 0, jnp.where(two == most, one, one + two))
    inner = jnp.where(one == most, two, one)
    facts_ref[0] = core
    facts_ref[1] = jnp.where(core == 0, longest & (half - 1), 0)
    facts_ref[2] = jnp.where(core == 0, 0, inner)
    facts_ref[3] = longest


def split_scale(scale):
    high = scale.astype(BF16).astype(F32)
    rest = scale - high
    middle = rest.astype(BF16).astype(F32)
    return high, middle, rest - middle


def fetch_kernel(
    incoming_ref, upper_ref, table_hbm, scale_hbm, out_hbm, lower_ref, scale_ref, out_ref, sems, scale_sem, out_sems
):
    scale_load = pltpu.make_async_copy(scale_hbm, scale_ref, scale_sem)
    scale_load.start()
    upper, width = upper_ref.shape
    loads = parts_of(table_hbm, lower_ref, sems, upper, 0)
    size = scale_ref.shape[1]
    slots = out_ref.shape[0] * CAPACITY
    devices = slots // CAPACITY
    device_of = iota((slots, devices), 0) >> 1 == iota((slots, devices), 1)
    spread = jnp.where(device_of, 1.0, 0.0).astype(BF16)
    wanted = incoming_ref[...]
    high = nn_dot(spread, (wanted >> 4).astype(F32).astype(BF16))
    low = nn_dot(spread, (wanted & 15).astype(F32).astype(BF16))
    mine = iota((slots, 128), 1) == (iota((slots, 128), 0) & 1)
    row = jnp.sum(jnp.where(mine, high * 16.0 + low, 0.0), axis=1, keepdims=True)
    chosen = row.astype(I32) - 1 == iota((slots, size), 1)
    hot = jnp.where(chosen, 1.0, 0.0).astype(BF16)
    scale_load.wait()
    scale = jnp.sum(jnp.where(chosen, scale_ref[...], 0.0), axis=1, keepdims=True)
    high, middle, low = split_scale(scale)
    lane = iota((slots, 128), 1)
    pieces = jnp.where(
        lane == 0, high, jnp.where(lane == 1, middle, jnp.where(lane == 2, low, 0.0))
    )
    out_ref[:, :, width : width + 128] = pieces.astype(BF16).reshape(devices, CAPACITY, 128)
    for load in loads:
        load.wait()
    stores = []
    for base in range(0, width, 256):
        columns = slice(base, base + 256)
        rows = nn_dot(hot[:, :upper], upper_ref[:, columns])
        rows += nn_dot(hot[:, upper:], lower_ref[:, columns])
        out_ref[:, :, columns] = rows.astype(BF16).reshape(devices, CAPACITY, 256)
        columns = slice(base, base + 256 if base + 256 < width else width + 128)
        stores.append(
            pltpu.make_async_copy(
                out_ref.at[:, :, columns], out_hbm.at[:, :, columns], out_sems.at[base // 256]
            )
        )
        stores[-1].start()
    for store in stores:
        store.wait()


def mix_kernel(cot_ref, weight_ref, out_ref):
    out_ref[...] = nt_dot(cot_ref[...], weight_ref[...])


def output_kernel(embed_ref, mixed_ref, weight_ref, out_ref):
    out_ref[...] = (embed_ref[...] + nn_dot(mixed_ref[...], weight_ref[...])).astype(BF16)


def project_kernel(
    returned_ref, slot_ref, mixed_ref, weight_hbm, packed_ref, proj_ref, embed_ref, gate_ref, weight_ref, sems
):
    width = embed_ref.shape[1]
    loads = parts_of(weight_hbm, weight_ref, sems, 0, 1)
    heads = packed_ref.shape[0]
    devices, capacity, wide = returned_ref.shape
    slots, rows = devices * capacity, slot_ref.shape[1]
    place = jnp.where(slot_ref[...] == iota((slots, rows), 0), 1.0, 0.0).astype(BF16)
    total = tn_dot(place, returned_ref[...].reshape(slots, wide))
    scale = total[:, width : width + 1] + (
        total[:, width + 1 : width + 2] + total[:, width + 2 : width + 3]
    )
    embedded = total[:, :width] * scale
    embed_ref[...] = embedded
    normed = normalize(embedded)[0].astype(BF16)
    for t in range(4):
        loads[t].wait()
        for pair in range(heads // 2):
            columns = slice(pair * 256, (pair + 1) * 256)
            base = t * width + pair * 256
            projected = nn_dot(normed, weight_ref[:, base : base + 256])
            proj_ref[:, base : base + 256] = projected
            active = silu_parts(0.5 * projected)[1].astype(BF16)
            if t == 0:
                gate_ref[:, columns] = active
                active = (active.astype(F32) * mixed_ref[:, columns]).astype(BF16)
            for i in range(2):
                packed_ref[2 * pair + i, :, t * 128 : (t + 1) * 128] = active[
                    :, i * 128 : (i + 1) * 128
                ]


def upper_rows(facts, core, s, shape):
    rows = shape[0]
    residue = s * 2 * rows + core * rows + iota(shape, 0)
    return (jnp.where(residue >= facts[3], 1, 0) ^ facts[0]) == 1


def choose(mask, yes, no):
    return jnp.where(mask, yes, no)


def join_kernel(facts, mine_ref, received_ref, out_ref):
    quarter = mine_ref.shape[0]
    for s in range(quarter):
        upper = upper_rows(facts, facts[0], s, mine_ref.shape[1:])
        out_ref[s] = choose(upper, mine_ref[s], received_ref[s])
        out_ref[s + quarter] = choose(upper, received_ref[s], mine_ref[s])


def rows_of(facts, s, side, rows, half):
    start = ((s - facts[1] // TILE) & (half // TILE - 1)) * TILE + side * rows
    return pl.ds(pl.multiple_of(start, rows), rows)


def share_of(facts, query_base, keys, half):
    seam, bound = facts[1] & (TILE - 1), facts[2]
    place = (query_base + iota((1, TILE), 1) - seam) & (half - 1)
    later = place >= bound
    first = jnp.where(later, bound, 0)
    inv_length = 1.0 / jnp.where(later, half - bound, bound).astype(F32)
    at = (iota((keys, 1), 0) - seam) & (half - 1)
    return jnp.where((at <= place) & (at >= first), inv_length, 0.0)


def blocks_of(half):
    for base in range(0, half, TILE):
        yield base, (half if base == 0 else base + TILE)


def attend_kernel(
    facts, x_ref, received_ref, y_ref, att_ref, grad_ref, stats_ref, turned
):
    core = facts[0]
    half, lanes = y_ref.shape
    heads, rows = received_ref.shape[0], received_ref.shape[1]
    quarter = heads // 2
    hdim = att_ref.shape[0]
    for s in range(quarter):
        for ref, side in ((x_ref, core), (received_ref, 1 - core)):
            upper = upper_rows(facts, side, s, (rows, lanes))
            y_ref[rows_of(facts, s, side, rows, half), :] = choose(upper, ref[s], ref[s + quarter])
    for base in range(0, half, TILE):
        span = slice(base, base + TILE)
        grad_ref[:, span] = y_ref[span, 0:128].astype(F32).T.astype(BF16)
        turned[:, span] = y_ref[span, 128:256].astype(F32).T.astype(BF16)
    for base, keys in blocks_of(half):
        span = slice(base, base + TILE)
        half_scores = nt_dot(y_ref[0:keys, 384:512], y_ref[span, 256:384]) * (0.5 * hdim**-0.5)
        weights = (silu_parts(half_scores)[1] * share_of(facts, base, keys, half)).astype(BF16)
        attention = nn_dot(turned[:, 0:keys], weights)
        att_ref[:, span] = attention
        gated = grad_ref[:, span].astype(F32)
        center = jnp.mean(attention, axis=0, keepdims=True)
        shifted = attention - center
        lines = [
            center,
            jnp.sum(shifted * shifted, axis=0, keepdims=True),
            jnp.sum(gated, axis=0, keepdims=True),
            jnp.sum(gated * shifted, axis=0, keepdims=True),
        ]
        line = iota((8, TILE), 0)
        table = jnp.zeros((8, TILE), F32)
        for i, values in enumerate(lines):
            table = jnp.where(line == i, values, table)
        for h in range(heads):
            stats_ref[h, :, span] = table[0:4]


def backward_kernel(
    facts, y_ref, att_ref, gated_ref, stats_ref, mine_ref, send_ref, attn, grad, dq, dk, dv
):
    core = facts[0]
    half = y_ref.shape[0]
    heads = stats_ref.shape[0]
    quarter, rows = mine_ref.shape[0], mine_ref.shape[1]
    hdim = att_ref.shape[0]
    width = heads * hdim
    stat = [[stats_ref[h, i : i + 1, :] for i in range(4)] for h in range(heads)]
    mean = sum(s[0] for s in stat) / heads
    variance, mean_grad, mean_prod = 0.0, 0.0, 0.0
    for center, spread, grad_sum, prod_sum in stat:
        offset = center - mean
        variance += spread + hdim * offset * offset
        mean_grad += grad_sum
        mean_prod += prod_sum + offset * grad_sum
    inv_attn = lax.rsqrt(variance / width + EPSILON)
    mean_grad = mean_grad / width
    mean_prod = inv_attn * mean_prod / width
    for base in range(0, half, TILE):
        span = slice(base, base + TILE)
        inv = inv_attn[:, span]
        attn_norm = (att_ref[:, span] - mean[:, span]) * inv
        attn[span, :] = attn_norm.T.astype(BF16)
        gated = gated_ref[:, span].astype(F32)
        grad[:, span] = (
            inv * (gated - mean_grad[:, span] - attn_norm * mean_prod[:, span])
        ).astype(BF16)
    scaling = 0.5 * hdim**-0.5
    for base, keys in blocks_of(half):
        span = slice(base, base + TILE)
        key, query, grad_out = y_ref[0:keys, 384:512], y_ref[span, 256:384], grad[:, span]
        share = share_of(facts, base, keys, half)
        twice, product = silu_parts(nt_dot(key, query) * scaling)
        weights = (product * share).astype(BF16)
        slope = (twice + product * (2.0 - twice)) * share
        grad_scores = (nn_dot(y_ref[0:keys, 128:256], grad_out) * slope).astype(BF16)
        grad_value = nt_dot(weights, grad_out)
        grad_key = nn_dot(grad_scores, query)
        dq[span, :] = (tn_dot(grad_scores, key) * scaling).astype(BF16)
        if base == 0:
            dv[...] = grad_value
            dk[...] = grad_key
        else:
            dv[0:keys, :] += grad_value
            dk[0:keys, :] += grad_key
    for s in range(quarter):
        for out_ref, side in ((mine_ref, core), (send_ref, 1 - core)):
            at = rows_of(facts, s, side, rows, half)
            parts = (attn[at, :], dv[at, :], dq[at, :], dk[at, :] * scaling)
            for i, part in enumerate(parts):
                out_ref[s, :, i * hdim : (i + 1) * hdim] = part.astype(BF16)


def finish_kernel(
    back_ref, proj_ref, mixed_ref, gate_ref, slot_ref, embed_ref, cot_ref, weight_hbm, out_hbm, gated_hbm, weight_ref, gated_ref, out_ref, sems, sem, out_sems
):
    heads = back_ref.shape[0]
    width = embed_ref.shape[1]
    loads = parts_of(weight_hbm, weight_ref, sems, 0, 1)
    normed, inv_embed = normalize(embed_ref[...])
    cotangent = cot_ref[...].astype(F32)
    slots, rows = out_ref.shape[0] * out_ref.shape[1], slot_ref.shape[1]
    place = jnp.where(slot_ref[...] == iota((slots, rows), 0), 1.0, 0.0).astype(BF16)
    total = 0.0
    for t in range(4):
        for pair in range(heads // 2):
            if pair % 2 == 0:
                loads[2 * t + pair // 2].wait()
            columns = slice(pair * 256, (pair + 1) * 256)
            lanes = slice(t * 128, (t + 1) * 128)
            base = t * width + pair * 256
            grad_act = jnp.concatenate(
                [back_ref[2 * pair, :, lanes], back_ref[2 * pair + 1, :, lanes]], axis=1
            ).astype(F32)
            if t == 0:
                gated_ref[:, columns] = (grad_act * gate_ref[:, columns].astype(F32)).astype(BF16)
                grad_act = grad_act * mixed_ref[:, columns]
            projected = proj_ref[:, base : base + 256]
            twice, active = silu_parts(0.5 * projected)
            slope = 0.5 * (twice + active * (2.0 - twice))
            total += nt_dot((grad_act * slope).astype(BF16), weight_ref[:, base : base + 256])
    stores = [pltpu.make_async_copy(gated_ref, gated_hbm, sem)]
    stores[0].start()
    grad_embed = cotangent + normalize_back(total, normed, inv_embed)
    grad_embed = grad_embed.astype(BF16)
    for n in range(out_sems.shape[0]):
        step = width // out_sems.shape[0]
        columns = slice(n * step, (n + 1) * step)
        placed = nn_dot(place, grad_embed[:, columns]).astype(BF16)
        out_ref[:, :, columns] = placed.reshape(out_ref.shape[0], out_ref.shape[1], step)
        stores.append(
            pltpu.make_async_copy(
                out_ref.at[:, :, columns], out_hbm.at[:, :, columns], out_sems.at[n]
            )
        )
        stores[-1].start()
    for store in stores:
        store.wait()


def table_kernel(incoming_ref, arrived_ref, scale_ref, out_ref, buffer, sems):
    devices, capacity, width = arrived_ref.shape
    slots = devices * capacity
    arrived = arrived_ref[...].reshape(slots, width)
    steps = sems.shape[0]
    block = buffer.shape[0] // steps
    copies = []
    for n in range(steps):
        span = pl.ds(n * block, block)
        chosen = incoming_ref[...] - 1 - n * block == iota((block, slots), 0)
        total = nn_dot(jnp.where(chosen, 1.0, 0.0).astype(BF16), arrived)
        scale = jnp.broadcast_to(scale_ref[:, span], (128, block)).T
        buffer[span, :] = total * scale[:, 0:1]
        copies.append(pltpu.make_async_copy(buffer.at[span], out_ref.at[span], sems.at[n]))
        copies[-1].start()
    for copy in copies:
        copy.wait()


def per_device(
    table_rows,
    row_scales,
    owners,
    shard_rows,
    history_lengths,
    input_weight,
    output_weight,
    cotangent,
):
    rows = owners.shape[0]
    table_size, width = table_rows.shape
    heads = HEADS
    hdim = width // heads
    devices = lax.axis_size(("dp", "cp"))
    n_cp = lax.axis_size("cp")
    cores = n_cp // heads
    half = rows * n_cp // 2
    quarter = heads // 2
    slots = devices * CAPACITY
    groups = [[i * cores + c for i in range(heads)] for c in range(cores)]
    swap = [(i, i ^ 1) for i in range(n_cp)]
    core = (lax.axis_index("cp") % cores).reshape(1)
    everyone = ("dp", "cp")
    shape = jax.ShapeDtypeStruct
    smem = pl.BlockSpec(memory_space=pltpu.SMEM)
    vmem = pl.BlockSpec(memory_space=pltpu.VMEM)
    hbm = pl.BlockSpec(memory_space=pltpu.HBM)

    def kernel(body, name, ins, outs, out_shape, mib, scratch=()):
        return pl.pallas_call(
            body,
            in_specs=ins,
            out_specs=outs,
            out_shape=out_shape,
            scratch_shapes=list(scratch),
            compiler_params=pltpu.CompilerParams(vmem_limit_bytes=mib << 20 if mib else None),
            name=name,
        )

    def exchange(values, axes, **options):
        return lax.all_to_all(values, axes, split_axis=0, concat_axis=0, tiled=True, **options)

    def to_heads(values):
        return exchange(values, "cp", axis_index_groups=groups)

    def to_all(values):
        return exchange(values, everyone)

    dma = pltpu.SemaphoreType.DMA

    def far(values):
        return pltpu.with_memory_space_constraint(values, pltpu.HBM)

    def near(values):
        return pltpu.with_memory_space_constraint(values, pltpu.VMEM)

    weight_far = far(input_weight)
    scale_line = row_scales.reshape(1, table_size)
    requests, slot_line, facts = kernel(
        request_kernel,
        "request",
        [smem, smem, vmem, vmem],
        (vmem, vmem, smem),
        (shape((devices, 128), I32), shape((1, rows), I32), shape((4,), I32)),
        0,
    )(core, history_lengths, owners.reshape(1, rows), shard_rows.reshape(1, rows))
    incoming = exchange(requests.reshape(devices, 1, 128), everyone).reshape(devices, 128)

    wide = width + 128
    ahead = table_size * 5 // 8
    fetched = kernel(
        fetch_kernel,
        "fetch",
        [vmem, vmem, hbm, hbm],
        hbm,
        pltpu.HBM((devices, CAPACITY, wide), BF16),
        16,
        (
            pltpu.VMEM((table_size - ahead, width), BF16),
            pltpu.VMEM((1, table_size), F32),
            pltpu.VMEM((devices, CAPACITY, wide), BF16),
            dma((2,)),
            dma(()),
            dma((width // 256,)),
        ),
    )(incoming, near(table_rows[:ahead]), far(table_rows), far(scale_line))
    returned = to_all(fetched)

    output_far = far(output_weight)
    grad_mixed = kernel(
        mix_kernel, "mix", [vmem] * 2, vmem, shape((rows, width), F32), 8
    )(cotangent, output_far)

    near_weight = (pltpu.VMEM((width, 4 * width), BF16), dma((4,)))
    packed, projected, embedded, gate = kernel(
        project_kernel,
        "project",
        [vmem] * 3 + [hbm],
        (vmem, vmem, vmem, vmem),
        (
            shape((heads, rows, 4 * hdim), BF16),
            shape((rows, 4 * width), F32),
            shape((rows, width), F32),
            shape((rows, width), BF16),
        ),
        24,
        near_weight,
    )(returned, slot_line, grad_mixed, weight_far)

    branches = to_heads(packed)
    received = lax.ppermute(branches, "cp", swap)
    ordered, attention, gated, stats = kernel(
        attend_kernel,
        "attend",
        [smem, vmem, vmem],
        (vmem, vmem, vmem, vmem),
        (
            shape((half, 4 * hdim), BF16),
            shape((hdim, half), F32),
            shape((hdim, half), BF16),
            shape((heads, 4, half), F32),
        ),
        16,
        (pltpu.VMEM((hdim, half), BF16),),
    )(facts, branches, received)
    stats = to_heads(stats)

    backed = shape((quarter, rows, 4 * hdim), BF16)
    mine, send = kernel(
        backward_kernel,
        "backward",
        [smem, vmem, vmem, vmem, vmem],
        (vmem, vmem),
        (backed, backed),
        24,
        (
            pltpu.VMEM((half, hdim), BF16),
            pltpu.VMEM((hdim, half), BF16),
            pltpu.VMEM((half, hdim), BF16),
            pltpu.VMEM((half, hdim), F32),
            pltpu.VMEM((half, hdim), F32),
        ),
    )(facts, ordered, attention, gated, stats)
    received = lax.ppermute(send, "cp", swap)
    joined = kernel(
        join_kernel,
        "join",
        [smem, vmem, vmem],
        vmem,
        shape((heads, rows, 4 * hdim), BF16),
        8,
    )(facts, mine, received)
    back = to_heads(joined)

    outgoing, mixed = kernel(
        finish_kernel,
        "finish",
        [vmem] * 7 + [hbm],
        (hbm, hbm),
        (pltpu.HBM((devices, CAPACITY, width), BF16), pltpu.HBM((rows, width), BF16)),
        24,
        (
            near_weight[0],
            pltpu.VMEM((rows, width), BF16),
            pltpu.VMEM((devices, CAPACITY, width), BF16),
            dma((8,)),
            dma(()),
            dma((2,)),
        ),
    )(back, projected, grad_mixed, gate, slot_line, embedded, cotangent, weight_far)
    arrived = to_all(outgoing)
    layer_out = kernel(
        output_kernel, "output", [vmem] * 3, vmem, shape((rows, width), BF16), 8
    )(embedded, mixed, output_far)

    table_grad = kernel(
        table_kernel,
        "table",
        [vmem] * 3,
        hbm,
        shape((table_size, width), F32),
        24,
        (pltpu.VMEM((table_size, width), F32), pltpu.SemaphoreType.DMA((16,))),
    )(incoming[:, :CAPACITY].reshape(1, slots), arrived, scale_line)
    return (layer_out, table_grad)


def solution(mesh):
    return jax.shard_map(
        per_device,
        mesh=mesh,
        in_specs=(
            P(("dp", "cp"), None),
            P(("dp", "cp")),
            P(("dp", "cp"), None),
            P(("dp", "cp")),
            P("dp", None),
            P(),
            P(),
            P(("dp", "cp"), None),
        ),
        out_specs=(P(("dp", "cp"), None), P(("dp", "cp"), None)),
        check_vma=False,
    )
```
